32 devices in a mesh: ens: 4 (over z), gx: 2 (over x), gy: 4 (over y, core).
Axes of the slice: x: 2, y: 2, z: 4, core: 2. Of those that a mesh axis runs over, the one named last changes fastest.
Arguments:
- members: bfloat16 [64, 75, 32, 512], P(('ens', 'gx'), None, None, 'gy'), may hold values from -0.75 to 0.75
- spread: bfloat16 [75, 75], replicated, as said below
- sea_mask: int32 [32, 512], P(('ens', 'gx'), 'gy'), may hold values 0 or 1
- innovations: float32 [75, 32, 512], P(None, ('ens', 'gx'), 'gy'), may hold values from -19 to 19
- obs_error: float32 [75, 32, 512], P(None, ('ens', 'gx'), 'gy'), may hold values from 0.3 to 3
- static_scale: float32 [75, 32, 512], P(None, ('ens', 'gx'), 'gy'), may hold values from 2 to 8
Outputs:
- increment: float32 [75, 32, 512], P(None, ('ens', 'gx'), 'gy')
- alpha_fields: bfloat16 [64, 75, 32, 512], P(('ens', 'gx'), None, None, 'gy')
The draws below stay inside these ranges and needn't reach their ends.
Inputs may be any that keep to these rules, and one draw needn't show every extreme that they name: `spread`: symmetric and positive definite. `sea_mask`: 1 marks sea, 0 land.
All inputs are finite; a program needn't handle non-finite values. No bound on the sum of `sea_mask` on one device may be relied on, other than what follows from the above.
Results may differ from the reference program's by a relative error of at most 0.0065.
Values may be sent and summed in bfloat16 or wider, within the bound.
A program may use at most 128 MiB of HBM per device.

```python
import math
import jax
import jax.numpy as jnp
from jax import lax

MEMBERS = 64
LAYERS = 75
GRIDS = 3
SWEEPS = 2
COARSE_SWEEPS = 4
ITERATIONS = 3
NX = 32
NY = 512


def draw_spread(key, part):
    noise = jax.random.uniform(key, (LAYERS, LAYERS), jnp.float32, -1.0, 1.0)
    symmetric = 0.45 * (noise + noise.T) / LAYERS
    leading = 1.0 + 0.5 * jax.random.uniform(jax.random.fold_in(key, 7), (LAYERS,), jnp.float32)
    identity = jnp.eye(LAYERS, dtype=jnp.float32)
    return (symmetric * (1.0 - identity) + identity * leading[:, None]).astype(jnp.bfloat16)


def draw_innovations(key, part):
    base = jnp.clip(jax.random.normal(key, (LAYERS, NX, NY), jnp.float32), -4.0, 4.0)
    rising = 3.0 ** (jnp.arange(NX, dtype=jnp.float32) / (NX - 1))
    return 0.5 * base * rising[None, :, None]


def place_ends(drawn, own_key, least, high):
    place = [jax.random.randint(jax.random.fold_in(own_key, axis), (), 0, length) for axis, length in enumerate(drawn.shape)]
    longest = drawn.shape.index(max(drawn.shape))
    neighbour = place[:longest] + [(place[longest] + 1) % drawn.shape[longest]] + place[longest + 1:]
    return drawn.at[tuple(place)].set(least).at[tuple(neighbour)].set(high)


def steps_of(stream_key, shape, cuts, low, top_value):
    factor_of = 1.0
    for axis_at, parts in cuts:
        steps = jax.random.uniform(jax.random.fold_in(jax.random.fold_in(stream_key, 6), axis_at), (parts,), jnp.float32, low / len(cuts), top_value / len(cuts))
        factor_of = factor_of * jnp.repeat(jnp.exp(steps), shape[axis_at] // parts).reshape((-1,) + (1,) * (len(shape) - 1 - axis_at))
    return factor_of


def normal_values(key, extent, deviation, limit, split=(), kind=jnp.bfloat16):
    level = steps_of(key, extent, split, -0.22, 0.18) if split else 1.0
    result = jax.random.normal(key, extent, jnp.float32) * deviation * level
    return jnp.minimum(jnp.maximum(result, -limit), limit).astype(kind)


def setup_inputs(seed: int = 0) -> dict:
    key_list = jax.random.split(jax.random.key(seed), 7)
    return {
        "members": normal_values(key_list[0], (MEMBERS, LAYERS, NX, NY), 0.125, 0.75, ((0, 8), (3, 4))),
        "spread": draw_spread(jax.random.fold_in(key_list[6], 71), 0),
        "sea_mask": place_ends((jax.random.randint(key_list[2], (NX, NY), 0, 8) < 7).astype(jnp.int32), jax.random.fold_in(key_list[2], 1), 0, 1),
        "innovations": draw_innovations(jax.random.fold_in(key_list[6], 71), 0),
        "obs_error": jnp.clip(jnp.exp(math.log(3.0) - 2.3025851 * jax.random.uniform(key_list[4], (LAYERS, NX, NY), jnp.float32) ** steps_of(key_list[4], (LAYERS, NX, NY), ((1, 8), (2, 4)), -0.2, 0.2)), 0.3, 3.0),
        "static_scale": jnp.clip(jnp.exp(math.log(8.0) - 1.3862944 * jax.random.uniform(key_list[5], (LAYERS, NX, NY), jnp.float32) ** steps_of(key_list[5], (LAYERS, NX, NY), ((1, 8), (2, 4)), -0.2, 0.2)), 2.0, 8.0),
    }


diffusivity = 16.0
damping = 0.8


def neighbours(values):
    padded = jnp.pad(values, ((0, 0), (1, 1), (1, 1)))
    return padded[:, 2:, 1:-1] + padded[:, :-2, 1:-1] + padded[:, 1:-1, 2:] + padded[:, 1:-1, :-2]


def apply_level(values, strength):
    return values + strength * (4.0 * values - neighbours(values))


def relax(values, source, strength):
    return values + damping * (source - apply_level(values, strength)) / (1.0 + 4.0 * strength)


def restrict(values):
    layer_count, row_count, column_count = values.shape
    return 0.25 * values.reshape(layer_count, row_count // 2, 2, column_count // 2, 2).sum(axis=(2, 4))


def prolong(values):
    layer_count, row_count, column_count = values.shape
    spread_out = jnp.broadcast_to(values[:, :, None, :, None], (layer_count, row_count, 2, column_count, 2))
    return spread_out.reshape(layer_count, 2 * row_count, 2 * column_count)


def vcycle(source, grid_level):
    strength = diffusivity / 4.0 ** grid_level
    solution = damping / (1.0 + 4.0 * strength) * source
    if grid_level == GRIDS - 1:
        for sweep_index in range(COARSE_SWEEPS - 1):
            solution = relax(solution, source, strength)
        return solution
    for sweep_index in range(SWEEPS - 1):
        solution = relax(solution, source, strength)
    remainder = source - apply_level(solution, strength)
    solution = solution + prolong(vcycle(restrict(remainder), grid_level + 1))
    for sweep_index in range(SWEEPS):
        solution = relax(solution, source, strength)
    return solution


def reference(members, spread, sea_mask, innovations, obs_error, static_scale):
    sea = sea_mask.astype(jnp.float32)[None]

    def member_mix(member, masked):
        product = (member.astype(jnp.float32) * masked).astype(jnp.bfloat16)
        flat = product.reshape(LAYERS, NX * NY)
        return jnp.dot(spread, flat, preferred_element_type=jnp.float32).reshape(LAYERS, NX, NY)

    def covariance(direction):
        masked = sea * direction

        def accumulate(running, member):
            return running + member.astype(jnp.float32) * member_mix(member, masked), None

        ensemble, unused = lax.scan(accumulate, jnp.zeros((LAYERS, NX, NY), jnp.float32), members)
        static = static_scale * vcycle(static_scale * masked, 0)
        return sea * (ensemble + static)

    weights = jnp.zeros((LAYERS, NX, NY), jnp.float32)
    increment = jnp.zeros((LAYERS, NX, NY), jnp.float32)
    residual = innovations
    direction = innovations
    norm_now = jnp.sum(residual * residual)
    for iteration in range(ITERATIONS):
        cov_dir = covariance(direction)
        image = cov_dir + obs_error * direction
        alpha = norm_now / jnp.sum(direction * image)
        weights = weights + alpha * direction
        increment = increment + alpha * cov_dir
        residual = residual - alpha * image
        norm_next = jnp.sum(residual * residual)
        direction = residual + (norm_next / norm_now) * direction
        norm_now = norm_next
    final_mask = sea * weights
    alpha_fields = lax.map(lambda member: member_mix(member, final_mask).astype(jnp.bfloat16), members)
    return increment, alpha_fields
```

```python
import functools
import math

import jax
import jax.numpy as jnp
from jax import lax
from jax.experimental import pallas as pl
from jax.experimental.pallas import tpu as pltpu
from jax.sharding import PartitionSpec as P

GRIDS = 3
SWEEPS = 2
COARSE_SWEEPS = 4
ITERATIONS = 3
SUB = 8
LANES = 128
PAIR = 2
TOGETHER = 8

diffusivity = 16.0
damping = 0.8
MESH = pl.DeviceIdType.MESH
F32 = jnp.float32
BF16 = jnp.bfloat16


def strength_of(level):
    return diffusivity / 4.0**level


def lane_index(width):
    return lax.broadcasted_iota(jnp.int32, (SUB, width), 1)


def over_rows(count, body):
    chunk = min(SUB, count)

    @pl.loop(0, count // chunk)
    def _(block):
        start = block * chunk
        for row in range(chunk):
            body(start + row)


def neighbours(ref, row, step):
    here = ref[row + 1]
    width = here.shape[-1]
    lane = lane_index(width)
    left = jnp.where(lane < step, 0.0, pltpu.roll(here, step, 1))
    right = jnp.where(lane >= width - step, 0.0, pltpu.roll(here, width - step, 1))
    return here, ref[row] + ref[row + 2] + left + right


def relax(src, source, dst, rows, level, scale=None):
    strength = strength_of(level)
    factor = damping / (1.0 + 4.0 * strength)

    def body(row):
        here, around = neighbours(src, row, 2**level)
        if scale is not None:
            here, around = here * scale, around * scale
        dst[row + 1] = (1.0 - damping) * here + factor * (source[row + 1] + strength * around)

    over_rows(rows, body)


def restrict_remainder(src, source, dst, rows, level):
    strength = strength_of(level)
    step = 2**level

    def one(row):
        here, around = neighbours(src, row, step)
        left_over = source[row + 1] - (1.0 + 4.0 * strength) * here + strength * around
        return left_over

    def body(row):
        both = one(2 * row) + one(2 * row + 1)
        width = both.shape[-1]
        even = lax.rem(lane_index(width) // step, 2) == 0
        other = jnp.where(even, pltpu.roll(both, width - step, 1), pltpu.roll(both, step, 1))
        dst[row + 1] = 0.25 * (both + other)

    over_rows(rows // 2, body)


def add_prolonged(dst, coarse, rows):
    def body(row):
        extra = coarse[row + 1]
        dst[2 * row + 1] = dst[2 * row + 1] + extra
        dst[2 * row + 2] = dst[2 * row + 2] + extra

    over_rows(rows // 2, body)


def vcycle(levels, level, rows):
    source, first, second = levels[level]
    factor = damping / (1.0 + 4.0 * strength_of(level))
    if level == GRIDS - 1:
        relax(source, source, first, rows, level, factor)
        for _ in range(COARSE_SWEEPS - 2):
            relax(first, source, second, rows, level)
            first, second = second, first
        return first
    relax(source, source, first, rows, level, factor)
    for _ in range(SWEEPS - 2):
        relax(first, source, second, rows, level)
        first, second = second, first
    restrict_remainder(first, source, levels[level + 1][0], rows, level)
    coarse = vcycle(levels, level + 1, rows // 2)
    add_prolonged(first, coarse, rows)
    for _ in range(SWEEPS):
        relax(first, source, second, rows, level)
        first, second = second, first
    return first


def kernel(
    sizes,
    groups,
    members,
    spread,
    sea,
    innovations,
    obs_error,
    scale,
    increment,
    alpha_fields,
    gathered,
    s_recv,
    e_recv,
    own_sum,
    residual,
    along,
    image,
    cov_dir,
    cov_res,
    ens_res,
    ens_along,
    f_along,
    f_send,
    f_recv,
    b_send,
    back,
    p_recv,
    state,
    blend,
    *rest,
):
    n_ens, n_gx, n_gy = sizes
    level_refs = rest[: 3 * GRIDS]
    (f_ssem, f_rsem, b_ssem, b_rsem, p_ssem, p_rsem, r_ssem, r_rsem, x_ssem, s_ssem, s_rsem, e_ssem, e_rsem) = rest[3 * GRIDS :]
    levels = [level_refs[3 * g : 3 * g + 3] for g in range(GRIDS)]
    n_blocks = n_ens * n_gx
    n_dev = n_blocks * n_gy
    spacing = n_dev // groups
    my_ens = lax.axis_index("ens")
    my_gx = lax.axis_index("gx")
    block = my_ens * n_gx + my_gx
    column = lax.axis_index("gy")
    me = block * n_gy + column
    is_owner = (lax.rem(me, spacing) == 0) & (me // spacing < groups)
    my_group = jnp.minimum(me // spacing, groups - 1)
    tile_rows = innovations.shape[0]
    layers = innovations.shape[1]
    count = members.shape[0]
    grid_rows = tile_rows * n_blocks
    parts = tile_rows // PAIR
    together = math.gcd(count, TOGETHER)

    def device(rank):
        return (rank // (n_gx * n_gy), lax.rem(rank // n_gy, n_gx), lax.rem(rank, n_gy))

    def ens_at(step):
        return lax.rem(my_ens + n_ens - step, n_ens)

    def gx_at(hop):
        return lax.rem(my_gx + hop, n_gx)

    def remote(src, dst, send_sem, recv_sem, target):
        pltpu.make_async_remote_copy(
            src_ref=src,
            dst_ref=dst,
            send_sem=send_sem,
            recv_sem=recv_sem,
            device_id=target,
            device_id_type=MESH,
        ).start()

    def send(src, dst, send_sem, recv_sem, rank):
        @pl.when(rank == me)
        def _():
            pltpu.make_async_copy(src, dst, recv_sem).start()

        @pl.when(rank != me)
        def _():
            remote(src, dst, send_sem, recv_sem, device(rank))

    def done(ref, sem):
        pltpu.make_async_copy(ref, ref, sem).wait()

    def sent(src, send_sem, rank):
        @pl.when(rank != me)
        def _():
            done(src, send_sem)

    barrier = pltpu.get_barrier_semaphore()

    @pl.loop(1, n_dev)
    def _(step):
        pl.semaphore_signal(
            barrier, inc=1, device_id=device(lax.rem(me + step, n_dev)), device_id_type=MESH
        )

    def pair_rows(pair):
        return pl.ds(pair * PAIR, PAIR)

    def tile_of(iteration, origin, pair):
        return gathered.at[iteration, origin, pair_rows(pair)]

    def part_of(origin, pair):
        return alpha_fields.at[0, pl.ds(origin * tile_rows + pair * PAIR, PAIR)]

    def forward_x(iteration, step, pair):
        origin = ens_at(step) * n_gx + my_gx
        tile = tile_of(iteration, origin, pair)
        for hop in range(1, n_gx):
            remote(
                tile,
                tile,
                x_ssem.at[step, hop, pair],
                r_rsem.at[iteration, origin, pair],
                (my_ens, gx_at(hop), column),
            )

    def receive_and_forward(iteration, step, pair):
        origin = ens_at(step) * n_gx + my_gx
        done(tile_of(iteration, origin, pair), r_rsem.at[iteration, origin, pair])
        forward_x(iteration, step, pair)

    def send_tile(iteration, pair):
        tile = tile_of(iteration, block, pair)
        for step in range(1, n_ens):
            remote(
                tile,
                tile,
                r_ssem.at[step, pair],
                r_rsem.at[iteration, block, pair],
                (ens_at(n_ens - step), my_gx, column),
            )
        forward_x(iteration, 0, pair)

    def tiles_sent(iteration):
        for pair in range(parts):
            for step in range(1, n_ens):
                done(tile_of(iteration, block, pair), r_ssem.at[step, pair])
            for step in range(n_ens):
                for hop in range(1, n_gx):
                    done(tile_of(iteration, block, pair), x_ssem.at[step, hop, pair])

    def sums_sent():
        for pair in range(parts):
            for step in range(n_ens):
                for hop in range(1, n_gx):
                    done(part_of(block, pair), s_ssem.at[step, hop, pair])
            for step in range(1, n_ens):
                done(part_of(block, pair), e_ssem.at[step, pair])

    def pack_source(pair, values):
        for group in range(groups):
            rows = [
                jnp.zeros((SUB, LANES), F32)
                if group * SUB + SUB > layers
                else value[group * SUB : (group + 1) * SUB]
                for value in values
            ]
            if group * SUB + SUB > layers:
                tail = jnp.zeros((group * SUB + SUB - layers, LANES), F32)
                rows = [jnp.concatenate([value[group * SUB :], tail], axis=0) for value in values]
            f_send[group, pair] = jnp.concatenate(rows, axis=0).astype(BF16)

    def send_source():
        @pl.loop(0, groups)
        def _(group):
            send(
                f_send.at[group],
                f_recv.at[pl.ds(block * parts, parts), column],
                f_ssem.at[group],
                f_rsem.at[me],
                group * spacing,
            )

    def source_sent():
        @pl.loop(0, groups)
        def _(group):
            sent(f_send.at[group], f_ssem.at[group], group * spacing)

    for r in range(tile_rows):
        start = innovations[r]
        residual[r] = start
        gathered[0, block, r] = (sea[r] * start).astype(BF16)
        zero = jnp.zeros_like(start)
        for ref in (along, image, cov_dir, ens_res, ens_along, increment):
            ref[r] = zero
    for pair in range(parts):
        rows = range(pair * PAIR, (pair + 1) * PAIR)
        pack_source(pair, [scale[r] * (sea[r] * innovations[r]) for r in rows])
    blend[...] = jnp.zeros_like(blend)
    blend[1, 0] = jnp.ones((1, LANES), F32)
    state[0] = -jnp.ones((1, LANES), F32)
    state[1] = jnp.zeros((1, LANES), F32)
    state[2] = jnp.ones((1, LANES), F32)

    @pl.when(is_owner)
    def _():
        for refs in levels:
            for ref in refs:
                edge = jnp.zeros(ref.shape[1:], F32)
                ref[0] = edge
                ref[ref.shape[0] - 1] = edge

        @pl.loop(0, grid_rows)
        def _(row):
            f_along[row] = jnp.zeros(f_along.shape[1:], F32)
            levels[0][0][row + 1] = jnp.zeros(f_along.shape[1:], F32)

    pl.semaphore_wait(barrier, n_dev - 1)
    for pair in range(parts):
        send_tile(0, pair)
    send_source()

    def members_from(k, first):
        return [[members[k + n, first + r] for r in range(PAIR)] for n in range(together)]

    def mix(members_at, vector):
        product = [
            values * vector[r] for member in members_at for r, values in enumerate(member)
        ]
        mixed = jnp.dot(
            spread[...], jnp.concatenate(product, axis=1), preferred_element_type=F32
        )
        pieces = [mixed[:, n * LANES : (n + 1) * LANES] for n in range(len(product))]
        return [pieces[n : n + PAIR] for n in range(0, len(pieces), PAIR)]

    def partial_sum(iteration, origin, pair, store):
        vector = [gathered[iteration, origin, pair * PAIR + r] for r in range(PAIR)]
        first = origin * tile_rows + pair * PAIR

        def sum_of(k):
            values = members_from(k, first)
            mixed = mix(values, vector)
            sums = []
            for r in range(PAIR):
                running = values[0][r].astype(F32) * mixed[0][r]
                for n in range(1, together):
                    running = running + values[n][r].astype(F32) * mixed[n][r]
                sums.append(running)
            return sums

        sums = sum_of(0)
        for k in range(together, count, together):
            sums = [a + b for a, b in zip(sums, sum_of(k))]
        store(sums)

    def owner_cycle(iteration):
        @pl.loop(0, n_dev)
        def _(rank):
            blocks = pl.ds((rank // n_gy) * parts, parts)
            done(f_recv.at[blocks, lax.rem(rank, n_gy)], f_rsem.at[rank])

        source = levels[0][0]
        alpha, ratio = state[0], state[1]

        @pl.loop(0, grid_rows // PAIR)
        def _(pair):
            for c in range(n_gy):
                both = f_recv[pair, c].astype(F32)
                lanes = pl.ds(c * LANES, LANES)
                for r in range(PAIR):
                    row = pair * PAIR + r
                    more = both[r * SUB : (r + 1) * SUB] + ratio * f_along[row, :, lanes]
                    f_along[row, :, lanes] = more
                    source[row + 1, :, lanes] = source[row + 1, :, lanes] - alpha * more

        result = vcycle(levels, 0, grid_rows)

        @pl.when(iteration > 0)
        def _():
            cycle_sent()

        @pl.loop(0, grid_rows // PAIR)
        def _(pair):
            for c in range(n_gy):
                rows = [
                    result[pair * PAIR + r + 1, :, c * LANES : (c + 1) * LANES] for r in range(PAIR)
                ]
                b_send[pair, c] = jnp.concatenate(rows, axis=0).astype(BF16)

        @pl.loop(0, n_dev)
        def _(rank):
            blocks = pl.ds((rank // n_gy) * parts, parts)
            send(
                b_send.at[blocks, lax.rem(rank, n_gy)],
                back.at[my_group],
                b_ssem.at[rank],
                b_rsem.at[my_group],
                rank,
            )

    def cycle_sent():
        @pl.loop(0, n_dev)
        def _(rank):
            sent(back.at[0], b_ssem.at[rank], rank)

    def finish(iteration):
        @pl.loop(1, n_dev)
        def _(step):
            rank = lax.rem(me + step, n_dev)
            done(p_recv.at[iteration, rank], p_rsem.at[iteration, rank])
            done(p_recv.at[iteration, rank], p_ssem.at[step])

        sums = jnp.sum(jnp.sum(p_recv[iteration], axis=0), axis=1, keepdims=True)
        norm_next, product = (jnp.broadcast_to(sums[n : n + 1], (1, LANES)) for n in range(2))
        ratio = jnp.where(iteration == 0, 0.0, norm_next / state[2])
        alpha = norm_next / (product - ratio * norm_next / state[0])
        state[0] = alpha
        state[1] = ratio
        state[2] = norm_next
        for n in range(ITERATIONS):
            towards = ratio * blend[2, n] + blend[1, n]
            blend[2, n] = towards
            blend[3, n] = blend[3, n] + alpha * towards
            more = jnp.where(iteration + 1 == n, 1.0, 0.0) + ratio * blend[0, n]
            blend[0, n] = more
            blend[1, n] = blend[1, n] - alpha * more
        for r in range(tile_rows):
            more = image[r] + ratio * along[r]
            along[r] = more
            residual[r] = residual[r] - alpha * more
            cov = cov_res[r] + ratio * cov_dir[r]
            cov_dir[r] = cov
            increment[r] = increment[r] + alpha * cov

    def sum_x(step, pair):
        ens = ens_at(step)
        for hop in range(1, n_gx):
            gx = gx_at(hop)
            arrival = s_recv.at[gx, ens, pair_rows(pair)]
            done(arrival, s_rsem.at[gx, ens, pair])
            for r in range(PAIR):
                row = pair * PAIR + r
                own_sum[ens, row] = own_sum[ens, row] + s_recv[gx, ens, row].astype(F32)

        @pl.when(step > 0)
        def _():
            origin = ens * n_gx + my_gx
            for r in range(PAIR):
                row = pair * PAIR + r
                alpha_fields[0, origin * tile_rows + row] = own_sum[ens, row].astype(BF16)
            remote(
                part_of(origin, pair),
                e_recv.at[my_ens, pair_rows(pair)],
                e_ssem.at[step, pair],
                e_rsem.at[my_ens, pair],
                (ens, my_gx, column),
            )

    @pl.loop(0, ITERATIONS)
    def _(iteration):
        @pl.loop(1, n_ens)
        def _(step):
            receive_and_forward(iteration, step, 0)

        @pl.loop(0, parts * n_blocks)
        def _(job):
            pair = job // n_blocks
            inner = lax.rem(job, n_blocks)
            hop = inner // n_ens
            step = lax.rem(inner, n_ens)
            ens, gx = ens_at(step), gx_at(hop)
            origin = ens * n_gx + gx

            @pl.when((hop == 1) & (step > 0) & (pair < parts - 1))
            def _():
                receive_and_forward(iteration, step, pair + 1)

            @pl.when(hop > 0)
            def _():
                done(tile_of(iteration, origin, pair), r_rsem.at[iteration, origin, pair])

            def store(sums):
                @pl.when(hop == 0)
                def _():
                    for r in range(PAIR):
                        own_sum[ens, pair * PAIR + r] = sums[r]

                @pl.when(hop > 0)
                def _():
                    for r in range(PAIR):
                        alpha_fields[0, origin * tile_rows + pair * PAIR + r] = sums[r].astype(BF16)
                    remote(
                        part_of(origin, pair),
                        s_recv.at[my_gx, ens, pair_rows(pair)],
                        s_ssem.at[step, hop, pair],
                        s_rsem.at[my_gx, ens, pair],
                        (my_ens, gx, column),
                    )

            partial_sum(iteration, origin, pair, store)

            @pl.when((hop == n_gx - 1) & (pair > 0))
            def _():
                sum_x(step, pair - 1)

        @pl.when(iteration > 0)
        def _():
            finish(iteration - 1)

        @pl.when(is_owner)
        def _():
            owner_cycle(iteration)

        tiles_sent(iteration)
        source_sent()

        @pl.loop(0, n_ens)
        def _(step):
            sum_x(lax.rem(step + 1, n_ens), parts - 1)

        @pl.loop(0, groups)
        def _(group):
            done(back.at[group], b_rsem.at[group])

        alpha, ratio = state[0], state[1]
        own = jnp.zeros((1, LANES), F32)
        cross = jnp.zeros((1, LANES), F32)
        for pair in range(parts):
            for step in range(1, n_ens):
                ens = ens_at(step)
                done(e_recv.at[ens, pair_rows(pair)], e_rsem.at[ens, pair])
            static = [back[group, pair].astype(F32) for group in range(groups)]
            sources = []
            for r in range(PAIR):
                row = pair * PAIR + r
                cycled = jnp.concatenate(
                    [both[r * SUB : (r + 1) * SUB] for both in static], axis=0
                )[:layers]
                total = own_sum[my_ens, row]
                for step in range(1, n_ens):
                    total = total + e_recv[ens_at(step), row].astype(F32)
                more = total + ratio * ens_along[row]
                ens_along[row] = more
                ens = ens_res[row] - alpha * more
                ens_res[row] = ens
                cov = sea[row] * (ens + scale[row] * cycled)
                cov_res[row] = cov
                now = residual[row]
                img = cov + obs_error[row] * now
                image[row] = img
                masked = sea[row] * img
                sources.append(scale[row] * masked)
                own = own + jnp.sum(now * now, axis=0, keepdims=True)
                cross = cross + jnp.sum(now * img, axis=0, keepdims=True)

                @pl.when(iteration < ITERATIONS - 1)
                def _():
                    gathered[iteration + 1, block, row] = masked.astype(BF16)

            @pl.when(iteration < ITERATIONS - 1)
            def _():
                send_tile(iteration + 1, pair)

            pack_source(pair, sources)
        p_recv[iteration, me, 0:1] = own
        p_recv[iteration, me, 1:2] = cross

        @pl.when(iteration < ITERATIONS - 1)
        def _():
            send_source()

        @pl.loop(1, n_dev)
        def _(step):
            remote(
                p_recv.at[iteration, me],
                p_recv.at[iteration, me],
                p_ssem.at[step],
                p_rsem.at[iteration, me],
                device(lax.rem(me + step, n_dev)),
            )

        sums_sent()

    finish(ITERATIONS - 1)

    @pl.when(is_owner)
    def _():
        cycle_sent()

    @pl.loop(0, n_blocks * parts)
    def _(job):
        origin = job // parts
        pair = lax.rem(job, parts)
        vector = [
            sum(
                blend[3, n] * gathered[n, origin, pair * PAIR + r].astype(F32)
                for n in range(ITERATIONS)
            )
            for r in range(PAIR)
        ]
        first = origin * tile_rows + pair * PAIR
        for k in range(0, count, together):
            at = [[values.astype(F32) for values in member] for member in members_from(k, first)]
            product = [
                (values * vector[r]).astype(BF16) for member in at for r, values in enumerate(member)
            ]
            mixed = jnp.dot(
                spread[...], jnp.concatenate(product, axis=1), preferred_element_type=F32
            )
            for n in range(together):
                for r in range(PAIR):
                    at_lane = (n * PAIR + r) * LANES
                    alpha_fields[k + n, first + r] = mixed[:, at_lane : at_lane + LANES].astype(BF16)


def local(sizes, members, spread, sea_mask, innovations, obs_error, static_scale):
    n_ens, n_gx, n_gy = sizes
    n_blocks = n_ens * n_gx
    n_dev = n_blocks * n_gy
    count, layers, rows, lanes = members.shape
    tile_rows = innovations.shape[1]
    parts = tile_rows // PAIR
    groups = -(-layers // SUB)
    grid_rows = rows
    width = lanes * n_gy

    def field(values):
        return values.transpose(1, 0, 2)

    sea = sea_mask.astype(F32)[:, None, :]
    tile = (tile_rows, layers, lanes)
    f_tile = pltpu.VMEM(tile, F32)
    packed = (PAIR * SUB, lanes)
    scratch = [
        pltpu.VMEM((ITERATIONS, n_blocks, *tile), BF16),
        pltpu.VMEM((n_gx, n_ens, *tile), BF16),
        pltpu.VMEM((n_ens, *tile), BF16),
        pltpu.VMEM((n_ens, *tile), F32),
    ]
    scratch += [f_tile] * 7
    scratch += [
        pltpu.VMEM((grid_rows, SUB, width), F32),
        pltpu.VMEM((groups, parts, *packed), BF16),
        pltpu.VMEM((grid_rows // PAIR, n_gy, *packed), BF16),
        pltpu.VMEM((grid_rows // PAIR, n_gy, *packed), BF16),
        pltpu.VMEM((groups, parts, *packed), BF16),
        pltpu.VMEM((ITERATIONS, n_dev, 2, lanes), F32),
        pltpu.VMEM((3, 1, lanes), F32),
        pltpu.VMEM((4, ITERATIONS, 1, lanes), F32),
    ]
    for level in range(GRIDS):
        scratch += [pltpu.VMEM((grid_rows // 2**level + 2, SUB, width), F32)] * 3
    dma = pltpu.SemaphoreType.DMA
    scratch += [
        dma((groups,)),
        dma((n_dev,)),
        dma((n_dev,)),
        dma((groups,)),
        dma((n_dev,)),
        dma((ITERATIONS, n_dev)),
        dma((n_ens, parts)),
        dma((ITERATIONS, n_blocks, parts)),
        dma((n_ens, n_gx, parts)),
        dma((n_ens, n_gx, parts)),
        dma((n_gx, n_ens, parts)),
        dma((n_ens, parts)),
        dma((n_ens, parts)),
    ]
    vmem = pl.BlockSpec(memory_space=pltpu.VMEM)
    increment, alpha_fields = pl.pallas_call(
        functools.partial(kernel, sizes, groups),
        out_shape=(
            jax.ShapeDtypeStruct(tile, F32),
            jax.ShapeDtypeStruct((count, rows, layers, lanes), BF16),
        ),
        in_specs=[vmem] * 6,
        out_specs=(vmem, vmem),
        scratch_shapes=scratch,
        compiler_params=pltpu.CompilerParams(
            collective_id=0, has_side_effects=True, vmem_limit_bytes=65000 * 2**10
        ),
        name="window",
    )(members.transpose(0, 2, 1, 3), spread, sea, field(innovations), field(obs_error), field(static_scale))
    return increment.transpose(1, 0, 2), alpha_fields.transpose(0, 2, 1, 3)


def solution(mesh):
    in_specs = (
        P(("ens", "gx"), None, None, "gy"),
        P(),
        P(("ens", "gx"), "gy"),
        P(None, ("ens", "gx"), "gy"),
        P(None, ("ens", "gx"), "gy"),
        P(None, ("ens", "gx"), "gy"),
    )
    out_specs = (P(None, ("ens", "gx"), "gy"), P(("ens", "gx"), None, None, "gy"))
    sizes = tuple(mesh.shape[axis] for axis in ("ens", "gx", "gy"))
    return jax.shard_map(
        functools.partial(local, sizes),
        mesh=mesh,
        in_specs=in_specs,
        out_specs=out_specs,
        check_vma=False,
    )
```

```python
import functools
import math

import jax
import jax.numpy as jnp
from jax import lax
from jax.experimental import pallas as pl
from jax.experimental.pallas import tpu as pltpu
from jax.sharding import PartitionSpec as P

GRIDS = 3
SWEEPS = 2
COARSE_SWEEPS = 4
ITERATIONS = 3
SUB = 8
LANES = 128
PAIR = 2
ROWS = 4
HALF = SUB // 2
TOGETHER = 8

diffusivity = 16.0
damping = 0.8
MESH = pl.DeviceIdType.MESH
F32 = jnp.float32
BF16 = jnp.bfloat16


def strength_of(level):
    return diffusivity / 4.0**level


def lane_index(width):
    return lax.broadcasted_iota(jnp.int32, (SUB, width), 1)


def low_half(width):
    return lax.broadcasted_iota(jnp.int32, (SUB, width), 0) < HALF


def swapped(values):
    return pltpu.roll(values, HALF, 0)


def pack_rows(rows):
    low = low_half(LANES)
    firsts = [jnp.where(low, a, swapped(b)) for a, b in (rows[:2], rows[2:])]
    seconds = [jnp.where(low, swapped(a), b) for a, b in (rows[:2], rows[2:])]
    return [jnp.concatenate(blocks, axis=0).astype(BF16) for blocks in (firsts, seconds)]


def unpack_rows(firsts, seconds):
    low = low_half(LANES)
    firsts, seconds = firsts.astype(F32), seconds.astype(F32)
    rows = []
    for at in (0, SUB):
        a, c = firsts[at : at + SUB], seconds[at : at + SUB]
        rows += [jnp.where(low, a, swapped(c)), jnp.where(low, swapped(a), c)]
    return rows


def join_halves(ref, rows):
    low = low_half(ref.shape[-1])
    ref[0] = jnp.where(low, 0.0, swapped(ref[rows]))
    ref[rows + 1] = jnp.where(low, swapped(ref[1]), 0.0)


def over_rows(count, body):
    chunk = min(SUB, count)

    @pl.loop(0, count // chunk)
    def _(block):
        body(block * chunk, chunk)


def beside(here, step):
    width = here.shape[-1]
    lane = lane_index(width)
    left = jnp.where(lane < step, 0.0, pltpu.roll(here, step, 1))
    right = jnp.where(lane >= width - step, 0.0, pltpu.roll(here, width - step, 1))
    return left + right


def around(loaded, index, step):
    return loaded[index] + loaded[index + 2] + beside(loaded[index + 1], step)


def relax(load, source, dst, rows, level, scale=None):
    strength = strength_of(level)
    factor = damping / (1.0 + 4.0 * strength)
    keep = 1.0 - damping
    spread_by = factor * strength
    if scale is not None:
        keep, spread_by = keep * scale, spread_by * scale

    def body(start, chunk):
        loaded = load(start, chunk)
        for r in range(chunk):
            dst[start + r + 1] = (
                keep * loaded[r + 1]
                + factor * source[start + r + 1]
                + spread_by * around(loaded, r, 2**level)
            )

    over_rows(rows, body)
    join_halves(dst, rows)


def rows_of(ref):
    return lambda start, chunk: [ref[start + r] for r in range(chunk + 2)]


def prolonged(ref, coarse):
    def load(start, chunk):
        extra = [coarse[start // 2 + r] for r in range(chunk // 2 + 2)]
        return [ref[start + r] + extra[(r + 1) // 2] for r in range(chunk + 2)]

    return load


def restrict_remainder(src, source, dst, rows, level):
    strength = strength_of(level)
    step = 2**level

    def body(start, chunk):
        loaded = rows_of(src)(start, chunk)
        over = [
            source[start + r + 1]
            - (1.0 + 4.0 * strength) * loaded[r + 1]
            + strength * around(loaded, r, step)
            for r in range(chunk)
        ]
        for r in range(0, chunk, 2):
            both = over[r] + over[r + 1]
            width = both.shape[-1]
            even = lax.rem(lane_index(width) // step, 2) == 0
            other = jnp.where(even, pltpu.roll(both, width - step, 1), pltpu.roll(both, step, 1))
            dst[start // 2 + r // 2 + 1] = 0.25 * (both + other)

    over_rows(rows, body)
    join_halves(dst, rows // 2)


def vcycle(levels, level, rows):
    source, first, second = levels[level]
    factor = damping / (1.0 + 4.0 * strength_of(level))
    relax(rows_of(source), source, first, rows, level, factor)
    before = COARSE_SWEEPS - 2 if level == GRIDS - 1 else SWEEPS - 2
    for _ in range(before):
        relax(rows_of(first), source, second, rows, level)
        first, second = second, first
    if level == GRIDS - 1:
        return first
    restrict_remainder(first, source, levels[level + 1][0], rows, level)
    coarse = vcycle(levels, level + 1, rows // 2)
    load = prolonged(first, coarse)
    for _ in range(SWEEPS):
        relax(load, source, second, rows, level)
        first, second = second, first
        load = rows_of(first)
    return first


def kernel(
    sizes,
    groups,
    members,
    spread,
    sea,
    innovations,
    obs_error,
    scale,
    increment,
    alpha_fields,
    gathered,
    s_recv,
    e_recv,
    own_sum,
    residual,
    along,
    image,
    cov_dir,
    cov_res,
    ens_res,
    ens_along,
    f_along,
    f_send,
    f_recv,
    b_send,
    back,
    p_recv,
    state,
    blend,
    *rest,
):
    n_ens, n_gx, n_gy = sizes
    level_refs = rest[: 3 * GRIDS]
    (f_ssem, f_rsem, b_ssem, b_rsem, p_ssem, p_rsem, r_ssem, r_rsem, x_ssem, s_ssem, s_rsem, e_ssem, e_rsem) = rest[3 * GRIDS :]
    levels = [level_refs[3 * g : 3 * g + 3] for g in range(GRIDS)]
    n_blocks = n_ens * n_gx
    n_dev = n_blocks * n_gy
    my_ens = lax.axis_index("ens")
    my_gx = lax.axis_index("gx")
    block = my_ens * n_gx + my_gx
    column = lax.axis_index("gy")
    me = block * n_gy + column
    next_group = (me * groups + n_dev - 1) // n_dev
    is_owner = (next_group < groups) & (next_group * n_dev // groups == me)
    my_group = jnp.minimum(next_group, groups - 1)
    tile_rows = innovations.shape[0]
    layers = innovations.shape[1]
    count = members.shape[0]
    grid_rows = tile_rows * n_blocks
    half_rows = grid_rows // 2
    half_blocks = n_blocks // 2
    eights = -(-layers // SUB)
    quads = tile_rows // ROWS
    parts = tile_rows // PAIR
    together = math.gcd(count, TOGETHER)

    def device(rank):
        return (rank // (n_gx * n_gy), lax.rem(rank // n_gy, n_gx), lax.rem(rank, n_gy))

    def ens_at(step):
        return lax.rem(my_ens + n_ens - step, n_ens)

    def gx_at(hop):
        return lax.rem(my_gx + hop, n_gx)

    def remote(src, dst, send_sem, recv_sem, target):
        pltpu.make_async_remote_copy(
            src_ref=src,
            dst_ref=dst,
            send_sem=send_sem,
            recv_sem=recv_sem,
            device_id=target,
            device_id_type=MESH,
        ).start()

    def send(src, dst, send_sem, recv_sem, rank):
        @pl.when(rank == me)
        def _():
            pltpu.make_async_copy(src, dst, recv_sem).start()

        @pl.when(rank != me)
        def _():
            remote(src, dst, send_sem, recv_sem, device(rank))

    def done(ref, sem):
        pltpu.make_async_copy(ref, ref, sem).wait()

    def sent(src, send_sem, rank):
        @pl.when(rank != me)
        def _():
            done(src, send_sem)

    barrier = pltpu.get_barrier_semaphore()

    @pl.loop(1, n_dev)
    def _(step):
        pl.semaphore_signal(
            barrier, inc=1, device_id=device(lax.rem(me + step, n_dev)), device_id_type=MESH
        )

    def pair_rows(pair):
        return pl.ds(pair * PAIR, PAIR)

    def tile_of(iteration, origin, pair):
        return gathered.at[iteration, origin, pair_rows(pair)]

    def part_of(origin, pair):
        return alpha_fields.at[0, pl.ds(origin * tile_rows + pair * PAIR, PAIR)]

    def forward_x(iteration, step, pair):
        origin = ens_at(step) * n_gx + my_gx
        tile = tile_of(iteration, origin, pair)
        for hop in range(1, n_gx):
            remote(
                tile,
                tile,
                x_ssem.at[step, hop, pair],
                r_rsem.at[iteration, origin, pair],
                (my_ens, gx_at(hop), column),
            )

    def receive_and_forward(iteration, step, pair):
        origin = ens_at(step) * n_gx + my_gx
        done(tile_of(iteration, origin, pair), r_rsem.at[iteration, origin, pair])
        forward_x(iteration, step, pair)

    def send_tile(iteration, pair):
        tile = tile_of(iteration, block, pair)
        for step in range(1, n_ens):
            remote(
                tile,
                tile,
                r_ssem.at[step, pair],
                r_rsem.at[iteration, block, pair],
                (ens_at(n_ens - step), my_gx, column),
            )
        forward_x(iteration, 0, pair)

    def tiles_sent(iteration):
        for pair in range(parts):
            for step in range(1, n_ens):
                done(tile_of(iteration, block, pair), r_ssem.at[step, pair])
            for step in range(n_ens):
                for hop in range(1, n_gx):
                    done(tile_of(iteration, block, pair), x_ssem.at[step, hop, pair])

    def sums_sent():
        for pair in range(parts):
            for step in range(n_ens):
                for hop in range(1, n_gx):
                    done(part_of(block, pair), s_ssem.at[step, hop, pair])
            for step in range(1, n_ens):
                done(part_of(block, pair), e_ssem.at[step, pair])

    def pack_source(values):
        for eight in range(eights):
            rows = [value[eight * SUB : (eight + 1) * SUB] for value in values]
            if eight * SUB + SUB > layers:
                tail = jnp.zeros((eight * SUB + SUB - layers, LANES), F32)
                rows = [jnp.concatenate([row, tail], axis=0) for row in rows]
            for quad in range(quads):
                blocks = pack_rows(rows[quad * ROWS : (quad + 1) * ROWS])
                for n, packed in enumerate(blocks):
                    f_send[2 * eight + n, quad] = packed

    def send_source():
        @pl.loop(0, groups)
        def _(group):
            send(
                f_send.at[group],
                f_recv.at[pl.ds(block * quads, quads), column],
                f_ssem.at[group],
                f_rsem.at[me],
                group * n_dev // groups,
            )

    def source_sent():
        @pl.loop(0, groups)
        def _(group):
            sent(f_send.at[group], f_ssem.at[group], group * n_dev // groups)

    for r in range(tile_rows):
        start = innovations[r]
        residual[r] = start
        gathered[0, block, r] = (sea[r] * start).astype(BF16)
        zero = jnp.zeros_like(start)
        for ref in (along, image, cov_dir, ens_res, ens_along, increment):
            ref[r] = zero
    pack_source([scale[r] * (sea[r] * innovations[r]) for r in range(tile_rows)])
    for group in range(groups, 2 * eights):
        back[group] = jnp.zeros(back.shape[1:], BF16)
    blend[...] = jnp.zeros_like(blend)
    blend[1, 0] = jnp.ones((1, LANES), F32)
    state[0] = -jnp.ones((1, LANES), F32)
    state[1] = jnp.zeros((1, LANES), F32)
    state[2] = jnp.ones((1, LANES), F32)

    @pl.when(is_owner)
    def _():
        @pl.loop(0, half_rows)
        def _(row):
            f_along[row] = jnp.zeros(f_along.shape[1:], F32)
            levels[0][0][row + 1] = jnp.zeros(f_along.shape[1:], F32)

    pl.semaphore_wait(barrier, n_dev - 1)
    for pair in range(parts):
        send_tile(0, pair)
    send_source()

    def members_from(k, first):
        return [[members[k + n, first + r] for r in range(PAIR)] for n in range(together)]

    def mix(members_at, vector):
        product = [
            values * vector[r] for member in members_at for r, values in enumerate(member)
        ]
        mixed = jnp.dot(
            spread[...], jnp.concatenate(product, axis=1), preferred_element_type=F32
        )
        pieces = [mixed[:, n * LANES : (n + 1) * LANES] for n in range(len(product))]
        return [pieces[n : n + PAIR] for n in range(0, len(pieces), PAIR)]

    def partial_sum(iteration, origin, pair, store):
        vector = [gathered[iteration, origin, pair * PAIR + r] for r in range(PAIR)]
        first = origin * tile_rows + pair * PAIR

        def sum_of(k):
            values = members_from(k, first)
            mixed = mix(values, vector)
            sums = []
            for r in range(PAIR):
                running = values[0][r].astype(F32) * mixed[0][r]
                for n in range(1, together):
                    running = running + values[n][r].astype(F32) * mixed[n][r]
                sums.append(running)
            return sums

        sums = sum_of(0)
        for k in range(together, count, together):
            sums = [a + b for a, b in zip(sums, sum_of(k))]
        store(sums)

    def owner_cycle(iteration):
        @pl.loop(0, n_dev)
        def _(rank):
            blocks = pl.ds((rank // n_gy) * quads, quads)
            done(f_recv.at[blocks, lax.rem(rank, n_gy)], f_rsem.at[rank])

        source = levels[0][0]
        alpha, ratio = state[0], state[1]

        @pl.loop(0, half_rows // ROWS)
        def _(quad):
            for c in range(n_gy):
                lanes = pl.ds(c * LANES, LANES)
                both = f_recv[quad, c], f_recv[half_blocks * quads + quad, c]
                for r, new in enumerate(unpack_rows(*both)):
                    row = quad * ROWS + r
                    more = new + ratio * f_along[row, :, lanes]
                    f_along[row, :, lanes] = more
                    source[row + 1, :, lanes] = source[row + 1, :, lanes] - alpha * more

        join_halves(source, half_rows)
        result = vcycle(levels, 0, half_rows)

        @pl.when(iteration > 0)
        def _():
            cycle_sent()

        @pl.loop(0, half_rows // ROWS)
        def _(quad):
            for c in range(n_gy):
                lanes = pl.ds(c * LANES, LANES)
                rows = [result[quad * ROWS + r + 1, :, lanes] for r in range(ROWS)]
                b_send[quad, c], b_send[half_blocks * quads + quad, c] = pack_rows(rows)

        @pl.loop(0, n_dev)
        def _(rank):
            blocks = pl.ds((rank // n_gy) * quads, quads)
            send(
                b_send.at[blocks, lax.rem(rank, n_gy)],
                back.at[my_group],
                b_ssem.at[rank],
                b_rsem.at[my_group],
                rank,
            )

    def cycle_sent():
        @pl.loop(0, n_dev)
        def _(rank):
            sent(back.at[0], b_ssem.at[rank], rank)

    def finish(iteration):
        @pl.loop(1, n_dev)
        def _(step):
            rank = lax.rem(me + step, n_dev)
            done(p_recv.at[iteration, rank], p_rsem.at[iteration, rank])
            done(p_recv.at[iteration, rank], p_ssem.at[step])

        sums = jnp.sum(jnp.sum(p_recv[iteration], axis=0), axis=1, keepdims=True)
        norm_next, product = (jnp.broadcast_to(sums[n : n + 1], (1, LANES)) for n in range(2))
        ratio = jnp.where(iteration == 0, 0.0, norm_next / state[2])
        alpha = norm_next / (product - ratio * norm_next / state[0])
        state[0] = alpha
        state[1] = ratio
        state[2] = norm_next
        for n in range(ITERATIONS):
            towards = ratio * blend[2, n] + blend[1, n]
            blend[2, n] = towards
            blend[3, n] = blend[3, n] + alpha * towards
            more = jnp.where(iteration + 1 == n, 1.0, 0.0) + ratio * blend[0, n]
            blend[0, n] = more
            blend[1, n] = blend[1, n] - alpha * more
        for r in range(tile_rows):
            more = image[r] + ratio * along[r]
            along[r] = more
            residual[r] = residual[r] - alpha * more
            cov = cov_res[r] + ratio * cov_dir[r]
            cov_dir[r] = cov
            increment[r] = increment[r] + alpha * cov

    def sum_x(step, pair):
        ens = ens_at(step)
        for hop in range(1, n_gx):
            gx = gx_at(hop)
            arrival = s_recv.at[gx, ens, pair_rows(pair)]
            done(arrival, s_rsem.at[gx, ens, pair])
            for r in range(PAIR):
                row = pair * PAIR + r
                own_sum[ens, row] = own_sum[ens, row] + s_recv[gx, ens, row].astype(F32)

        @pl.when(step > 0)
        def _():
            origin = ens * n_gx + my_gx
            for r in range(PAIR):
                row = pair * PAIR + r
                alpha_fields[0, origin * tile_rows + row] = own_sum[ens, row].astype(BF16)
            remote(
                part_of(origin, pair),
                e_recv.at[my_ens, pair_rows(pair)],
                e_ssem.at[step, pair],
                e_rsem.at[my_ens, pair],
                (ens, my_gx, column),
            )

    @pl.loop(0, ITERATIONS)
    def _(iteration):
        @pl.loop(1, n_ens)
        def _(step):
            receive_and_forward(iteration, step, 0)

        @pl.loop(0, parts * n_blocks)
        def _(job):
            pair = job // n_blocks
            inner = lax.rem(job, n_blocks)
            hop = inner // n_ens
            step = lax.rem(inner, n_ens)
            ens, gx = ens_at(step), gx_at(hop)
            origin = ens * n_gx + gx

            @pl.when((hop == 1) & (step > 0) & (pair < parts - 1))
            def _():
                receive_and_forward(iteration, step, pair + 1)

            @pl.when(hop > 0)
            def _():
                done(tile_of(iteration, origin, pair), r_rsem.at[iteration, origin, pair])

            def store(sums):
                @pl.when(hop == 0)
                def _():
                    for r in range(PAIR):
                        own_sum[ens, pair * PAIR + r] = sums[r]

                @pl.when(hop > 0)
                def _():
                    for r in range(PAIR):
                        alpha_fields[0, origin * tile_rows + pair * PAIR + r] = sums[r].astype(BF16)
                    remote(
                        part_of(origin, pair),
                        s_recv.at[my_gx, ens, pair_rows(pair)],
                        s_ssem.at[step, hop, pair],
                        s_rsem.at[my_gx, ens, pair],
                        (my_ens, gx, column),
                    )

            partial_sum(iteration, origin, pair, store)

            @pl.when((hop == n_gx - 1) & (pair > 0))
            def _():
                sum_x(step, pair - 1)

        @pl.when(iteration > 0)
        def _():
            finish(iteration - 1)

        @pl.when(is_owner)
        def _():
            owner_cycle(iteration)

        tiles_sent(iteration)
        source_sent()

        @pl.loop(0, n_ens)
        def _(step):
            sum_x(lax.rem(step + 1, n_ens), parts - 1)

        @pl.loop(0, groups)
        def _(group):
            done(back.at[group], b_rsem.at[group])

        alpha, ratio = state[0], state[1]
        own = jnp.zeros((1, LANES), F32)
        cross = jnp.zeros((1, LANES), F32)
        cycled = [[] for _ in range(tile_rows)]
        for quad in range(quads):
            for eight in range(eights):
                rows = unpack_rows(back[2 * eight, quad], back[2 * eight + 1, quad])
                for r, row in enumerate(rows):
                    cycled[quad * ROWS + r].append(row)
        cycled = [jnp.concatenate(blocks, axis=0)[:layers] for blocks in cycled]
        sources = []
        for pair in range(parts):
            for step in range(1, n_ens):
                ens = ens_at(step)
                done(e_recv.at[ens, pair_rows(pair)], e_rsem.at[ens, pair])
            for r in range(PAIR):
                row = pair * PAIR + r
                total = own_sum[my_ens, row]
                for step in range(1, n_ens):
                    total = total + e_recv[ens_at(step), row].astype(F32)
                more = total + ratio * ens_along[row]
                ens_along[row] = more
                ens = ens_res[row] - alpha * more
                ens_res[row] = ens
                cov = sea[row] * (ens + scale[row] * cycled[row])
                cov_res[row] = cov
                now = residual[row]
                img = cov + obs_error[row] * now
                image[row] = img
                masked = sea[row] * img
                sources.append(scale[row] * masked)
                own = own + jnp.sum(now * now, axis=0, keepdims=True)
                cross = cross + jnp.sum(now * img, axis=0, keepdims=True)

                @pl.when(iteration < ITERATIONS - 1)
                def _():
                    gathered[iteration + 1, block, row] = masked.astype(BF16)

            @pl.when(iteration < ITERATIONS - 1)
            def _():
                send_tile(iteration + 1, pair)

        pack_source(sources)
        p_recv[iteration, me, 0:1] = own
        p_recv[iteration, me, 1:2] = cross

        @pl.when(iteration < ITERATIONS - 1)
        def _():
            send_source()

        @pl.loop(1, n_dev)
        def _(step):
            remote(
                p_recv.at[iteration, me],
                p_recv.at[iteration, me],
                p_ssem.at[step],
                p_rsem.at[iteration, me],
                device(lax.rem(me + step, n_dev)),
            )

        sums_sent()

    finish(ITERATIONS - 1)

    @pl.when(is_owner)
    def _():
        cycle_sent()

    @pl.loop(0, n_blocks * parts)
    def _(job):
        origin = job // parts
        pair = lax.rem(job, parts)
        vector = [
            sum(
                blend[3, n] * gathered[n, origin, pair * PAIR + r].astype(F32)
                for n in range(ITERATIONS)
            )
            for r in range(PAIR)
        ]
        first = origin * tile_rows + pair * PAIR
        for k in range(0, count, together):
            at = [[values.astype(F32) for values in member] for member in members_from(k, first)]
            product = [
                (values * vector[r]).astype(BF16) for member in at for r, values in enumerate(member)
            ]
            mixed = jnp.dot(
                spread[...], jnp.concatenate(product, axis=1), preferred_element_type=F32
            )
            for n in range(together):
                for r in range(PAIR):
                    at_lane = (n * PAIR + r) * LANES
                    alpha_fields[k + n, first + r] = mixed[:, at_lane : at_lane + LANES].astype(BF16)


def local(sizes, members, spread, sea_mask, innovations, obs_error, static_scale):
    n_ens, n_gx, n_gy = sizes
    n_blocks = n_ens * n_gx
    n_dev = n_blocks * n_gy
    count, layers, rows, lanes = members.shape
    tile_rows = innovations.shape[1]
    parts = tile_rows // PAIR
    half_rows = rows // 2
    groups = -(-layers // HALF)
    eights = -(-layers // SUB)
    quads = tile_rows // ROWS
    width = lanes * n_gy

    def field(values):
        return values.transpose(1, 0, 2)

    sea = sea_mask.astype(F32)[:, None, :]
    tile = (tile_rows, layers, lanes)
    f_tile = pltpu.VMEM(tile, F32)
    packed = (ROWS * HALF, lanes)
    scratch = [
        pltpu.VMEM((ITERATIONS, n_blocks, *tile), BF16),
        pltpu.VMEM((n_gx, n_ens, *tile), BF16),
        pltpu.VMEM((n_ens, *tile), BF16),
        pltpu.VMEM((n_ens, *tile), F32),
    ]
    scratch += [f_tile] * 7
    scratch += [
        pltpu.VMEM((half_rows, SUB, width), F32),
        pltpu.VMEM((2 * eights, quads, *packed), BF16),
        pltpu.VMEM((n_blocks * quads, n_gy, *packed), BF16),
        pltpu.VMEM((n_blocks * quads, n_gy, *packed), BF16),
        pltpu.VMEM((2 * eights, quads, *packed), BF16),
        pltpu.VMEM((ITERATIONS, n_dev, 2, lanes), F32),
        pltpu.VMEM((3, 1, lanes), F32),
        pltpu.VMEM((4, ITERATIONS, 1, lanes), F32),
    ]
    for level in range(GRIDS):
        scratch += [pltpu.VMEM((half_rows // 2**level + 2, SUB, width), F32)] * 3
    dma = pltpu.SemaphoreType.DMA
    scratch += [
        dma((groups,)),
        dma((n_dev,)),
        dma((n_dev,)),
        dma((groups,)),
        dma((n_dev,)),
        dma((ITERATIONS, n_dev)),
        dma((n_ens, parts)),
        dma((ITERATIONS, n_blocks, parts)),
        dma((n_ens, n_gx, parts)),
        dma((n_ens, n_gx, parts)),
        dma((n_gx, n_ens, parts)),
        dma((n_ens, parts)),
        dma((n_ens, parts)),
    ]
    vmem = pl.BlockSpec(memory_space=pltpu.VMEM)
    increment, alpha_fields = pl.pallas_call(
        functools.partial(kernel, sizes, groups),
        out_shape=(
            jax.ShapeDtypeStruct(tile, F32),
            jax.ShapeDtypeStruct((count, rows, layers, lanes), BF16),
        ),
        in_specs=[vmem] * 6,
        out_specs=(vmem, vmem),
        scratch_shapes=scratch,
        compiler_params=pltpu.CompilerParams(
            collective_id=0, has_side_effects=True, vmem_limit_bytes=64000 * 2**10
        ),
        name="window",
    )(members.transpose(0, 2, 1, 3), spread, sea, field(innovations), field(obs_error), field(static_scale))
    return increment.transpose(1, 0, 2), alpha_fields.transpose(0, 2, 1, 3)


def solution(mesh):
    in_specs = (
        P(("ens", "gx"), None, None, "gy"),
        P(),
        P(("ens", "gx"), "gy"),
        P(None, ("ens", "gx"), "gy"),
        P(None, ("ens", "gx"), "gy"),
        P(None, ("ens", "gx"), "gy"),
    )
    out_specs = (P(None, ("ens", "gx"), "gy"), P(("ens", "gx"), None, None, "gy"))
    sizes = tuple(mesh.shape[axis] for axis in ("ens", "gx", "gy"))
    return jax.shard_map(
        functools.partial(local, sizes),
        mesh=mesh,
        in_specs=in_specs,
        out_specs=out_specs,
        check_vma=False,
    )
```

```python
import functools
import math

import jax
import jax.numpy as jnp
from jax import lax
from jax.experimental import pallas as pl
from jax.experimental.pallas import tpu as pltpu
from jax.sharding import PartitionSpec as P

GRIDS = 3
SWEEPS = 2
COARSE_SWEEPS = 4
ITERATIONS = 3
SUB = 8
LANES = 128
PAIR = 2
TURNED = 16
ROWS = 4
HALF = SUB // 2
TOGETHER = 8

diffusivity = 16.0
damping = 0.8
MESH = pl.DeviceIdType.MESH
F32 = jnp.float32
BF16 = jnp.bfloat16


def strength_of(level):
    return diffusivity / 4.0**level


def lane_index(width):
    return lax.broadcasted_iota(jnp.int32, (SUB, width), 1)


def low_half(width):
    return lax.broadcasted_iota(jnp.int32, (SUB, width), 0) < HALF


def swapped(values):
    return pltpu.roll(values, HALF, 0)


def pack_rows(rows):
    low = low_half(LANES)
    firsts = [jnp.where(low, a, swapped(b)) for a, b in (rows[:2], rows[2:])]
    seconds = [jnp.where(low, swapped(a), b) for a, b in (rows[:2], rows[2:])]
    return [jnp.concatenate(blocks, axis=0).astype(BF16) for blocks in (firsts, seconds)]


def unpack_rows(firsts, seconds):
    low = low_half(LANES)
    firsts, seconds = firsts.astype(F32), seconds.astype(F32)
    rows = []
    for at in (0, SUB):
        a, c = firsts[at : at + SUB], seconds[at : at + SUB]
        rows += [jnp.where(low, a, swapped(c)), jnp.where(low, swapped(a), c)]
    return rows


def join_halves(ref, rows):
    low = low_half(ref.shape[-1])
    ref[0] = jnp.where(low, 0.0, swapped(ref[rows]))
    ref[rows + 1] = jnp.where(low, swapped(ref[1]), 0.0)


def over_rows(count, body):
    chunk = min(SUB, count)

    @pl.loop(0, count // chunk)
    def _(block):
        body(block * chunk, chunk)


def beside(here, step):
    width = here.shape[-1]
    lane = lane_index(width)
    left = jnp.where(lane < step, 0.0, pltpu.roll(here, step, 1))
    right = jnp.where(lane >= width - step, 0.0, pltpu.roll(here, width - step, 1))
    return left + right


def around(loaded, index, step):
    return loaded[index] + loaded[index + 2] + beside(loaded[index + 1], step)


def relax(load, source, dst, rows, level, scale=None):
    strength = strength_of(level)
    factor = damping / (1.0 + 4.0 * strength)
    keep = 1.0 - damping
    spread_by = factor * strength
    if scale is not None:
        keep, spread_by = keep * scale, spread_by * scale

    def body(start, chunk):
        loaded = load(start, chunk)
        for r in range(chunk):
            dst[start + r + 1] = (
                keep * loaded[r + 1]
                + factor * source[start + r + 1]
                + spread_by * around(loaded, r, 2**level)
            )

    over_rows(rows, body)
    join_halves(dst, rows)


def rows_of(ref):
    return lambda start, chunk: [ref[start + r] for r in range(chunk + 2)]


def prolonged(ref, coarse):
    def load(start, chunk):
        extra = [coarse[start // 2 + r] for r in range(chunk // 2 + 2)]
        return [ref[start + r] + extra[(r + 1) // 2] for r in range(chunk + 2)]

    return load


def restrict_remainder(src, source, dst, rows, level):
    strength = strength_of(level)
    step = 2**level

    def body(start, chunk):
        loaded = rows_of(src)(start, chunk)
        over = [
            source[start + r + 1]
            - (1.0 + 4.0 * strength) * loaded[r + 1]
            + strength * around(loaded, r, step)
            for r in range(chunk)
        ]
        for r in range(0, chunk, 2):
            both = over[r] + over[r + 1]
            width = both.shape[-1]
            even = lax.rem(lane_index(width) // step, 2) == 0
            other = jnp.where(even, pltpu.roll(both, width - step, 1), pltpu.roll(both, step, 1))
            dst[start // 2 + r // 2 + 1] = 0.25 * (both + other)

    over_rows(rows, body)
    join_halves(dst, rows // 2)


def vcycle(levels, level, rows):
    source, first, second = levels[level]
    factor = damping / (1.0 + 4.0 * strength_of(level))
    relax(rows_of(source), source, first, rows, level, factor)
    before = COARSE_SWEEPS - 2 if level == GRIDS - 1 else SWEEPS - 2
    for _ in range(before):
        relax(rows_of(first), source, second, rows, level)
        first, second = second, first
    if level == GRIDS - 1:
        return first
    restrict_remainder(first, source, levels[level + 1][0], rows, level)
    coarse = vcycle(levels, level + 1, rows // 2)
    load = prolonged(first, coarse)
    for _ in range(SWEEPS):
        relax(load, source, second, rows, level)
        first, second = second, first
        load = rows_of(first)
    return first


def kernel(
    sizes,
    groups,
    members_in,
    spread,
    sea,
    innovations_in,
    obs_error_in,
    scale_in,
    increment,
    alpha_fields,
    innovations,
    obs_error,
    scale,
    members,
    native,
    turning,
    gathered,
    s_recv,
    e_recv,
    own_sum,
    residual,
    along,
    image,
    cov_dir,
    cov_res,
    ens_res,
    ens_along,
    f_along,
    f_send,
    f_recv,
    b_send,
    back,
    p_recv,
    state,
    blend,
    *rest,
):
    n_ens, n_gx, n_gy = sizes
    level_refs = rest[: 3 * GRIDS]
    (f_ssem, f_rsem, b_ssem, b_rsem, p_ssem, p_rsem, r_ssem, r_rsem, x_ssem, s_ssem, s_rsem, e_ssem, e_rsem, m_sem, i_sem) = rest[3 * GRIDS :]
    levels = [level_refs[3 * g : 3 * g + 3] for g in range(GRIDS)]
    n_blocks = n_ens * n_gx
    n_dev = n_blocks * n_gy
    my_ens = lax.axis_index("ens")
    my_gx = lax.axis_index("gx")
    block = my_ens * n_gx + my_gx
    column = lax.axis_index("gy")
    me = block * n_gy + column
    next_group = (me * groups + n_dev - 1) // n_dev
    is_owner = (next_group < groups) & (next_group * n_dev // groups == me)
    my_group = jnp.minimum(next_group, groups - 1)
    layers = spread.shape[0]
    tile_rows = innovations.shape[0]
    count = members.shape[0]
    grid_rows = tile_rows * n_blocks
    half_rows = grid_rows // 2
    half_blocks = n_blocks // 2
    eights = -(-layers // SUB)
    quads = tile_rows // ROWS
    parts = tile_rows // PAIR
    together = math.gcd(count, TOGETHER)

    def row_of(field, row):
        return field[row]

    def device(rank):
        return (rank // (n_gx * n_gy), lax.rem(rank // n_gy, n_gx), lax.rem(rank, n_gy))

    def ens_at(step):
        return lax.rem(my_ens + n_ens - step, n_ens)

    def gx_at(hop):
        return lax.rem(my_gx + hop, n_gx)

    def remote(src, dst, send_sem, recv_sem, target):
        pltpu.make_async_remote_copy(
            src_ref=src,
            dst_ref=dst,
            send_sem=send_sem,
            recv_sem=recv_sem,
            device_id=target,
            device_id_type=MESH,
        ).start()

    def send(src, dst, send_sem, recv_sem, rank):
        @pl.when(rank == me)
        def _():
            pltpu.make_async_copy(src, dst, recv_sem).start()

        @pl.when(rank != me)
        def _():
            remote(src, dst, send_sem, recv_sem, device(rank))

    def done(ref, sem):
        pltpu.make_async_copy(ref, ref, sem).wait()

    def sent(src, send_sem, rank):
        @pl.when(rank != me)
        def _():
            done(src, send_sem)

    def fetch(k):
        return pltpu.make_async_copy(members_in.at[k], native.at[k], m_sem.at[k])

    fields = [
        pltpu.make_async_copy(given.at[:, r, :], field.at[r], i_sem.at[n, r])
        for n, (given, field) in enumerate(
            ((innovations_in, innovations), (scale_in, scale), (obs_error_in, obs_error))
        )
        for r in range(tile_rows)
    ]
    for copy in fields:
        copy.start()

    @pl.loop(0, count)
    def _(k):
        fetch(k).start()

    barrier = pltpu.get_barrier_semaphore()

    @pl.loop(1, n_dev)
    def _(step):
        pl.semaphore_signal(
            barrier, inc=1, device_id=device(lax.rem(me + step, n_dev)), device_id_type=MESH
        )

    def pair_rows(pair):
        return pl.ds(pair * PAIR, PAIR)

    def tile_of(iteration, origin, pair):
        return gathered.at[iteration, origin, pair_rows(pair)]

    def part_of(origin, pair):
        return alpha_fields.at[0, pl.ds(origin * tile_rows + pair * PAIR, PAIR)]

    def forward_x(iteration, step, pair):
        origin = ens_at(step) * n_gx + my_gx
        tile = tile_of(iteration, origin, pair)
        for hop in range(1, n_gx):
            remote(
                tile,
                tile,
                x_ssem.at[step, hop, pair],
                r_rsem.at[iteration, origin, pair],
                (my_ens, gx_at(hop), column),
            )

    def receive_and_forward(iteration, step, pair):
        origin = ens_at(step) * n_gx + my_gx
        done(tile_of(iteration, origin, pair), r_rsem.at[iteration, origin, pair])
        forward_x(iteration, step, pair)

    def send_tile(iteration, pair):
        tile = tile_of(iteration, block, pair)
        for step in range(1, n_ens):
            remote(
                tile,
                tile,
                r_ssem.at[step, pair],
                r_rsem.at[iteration, block, pair],
                (ens_at(n_ens - step), my_gx, column),
            )
        forward_x(iteration, 0, pair)

    def tiles_sent(iteration):
        for pair in range(parts):
            for step in range(1, n_ens):
                done(tile_of(iteration, block, pair), r_ssem.at[step, pair])
            for step in range(n_ens):
                for hop in range(1, n_gx):
                    done(tile_of(iteration, block, pair), x_ssem.at[step, hop, pair])

    def sums_sent():
        for pair in range(parts):
            for step in range(n_ens):
                for hop in range(1, n_gx):
                    done(part_of(block, pair), s_ssem.at[step, hop, pair])
            for step in range(1, n_ens):
                done(part_of(block, pair), e_ssem.at[step, pair])

    def pack_source(values):
        for eight in range(eights):
            rows = [value[eight * SUB : (eight + 1) * SUB] for value in values]
            if eight * SUB + SUB > layers:
                tail = jnp.zeros((eight * SUB + SUB - layers, LANES), F32)
                rows = [jnp.concatenate([row, tail], axis=0) for row in rows]
            for quad in range(quads):
                blocks = pack_rows(rows[quad * ROWS : (quad + 1) * ROWS])
                for n, packed in enumerate(blocks):
                    f_send[2 * eight + n, quad] = packed

    def send_source():
        @pl.loop(0, groups)
        def _(group):
            send(
                f_send.at[group],
                f_recv.at[pl.ds(block * quads, quads), column],
                f_ssem.at[group],
                f_rsem.at[me],
                group * n_dev // groups,
            )

    def source_sent():
        @pl.loop(0, groups)
        def _(group):
            sent(f_send.at[group], f_ssem.at[group], group * n_dev // groups)

    for copy in fields:
        copy.wait()
    for r in range(tile_rows):
        start = row_of(innovations, r)
        residual[r] = start
        gathered[0, block, r] = (sea[r : r + 1].astype(F32) * start).astype(BF16)
        zero = jnp.zeros_like(start)
        for ref in (along, image, cov_dir, ens_res, ens_along, increment):
            ref[r] = zero
    pack_source([row_of(scale, r) * (sea[r : r + 1].astype(F32) * residual[r]) for r in range(tile_rows)])
    for group in range(groups, 2 * eights):
        back[group] = jnp.zeros(back.shape[1:], BF16)
    blend[...] = jnp.zeros_like(blend)
    blend[1, 0] = jnp.ones((1, LANES), F32)
    state[0] = -jnp.ones((1, LANES), F32)
    state[1] = jnp.zeros((1, LANES), F32)
    state[2] = jnp.ones((1, LANES), F32)

    @pl.when(is_owner)
    def _():
        @pl.loop(0, half_rows)
        def _(row):
            f_along[row] = jnp.zeros(f_along.shape[1:], F32)
            levels[0][0][row + 1] = jnp.zeros(f_along.shape[1:], F32)

    def turn(k):
        fetch(k).wait()

        @pl.loop(0, grid_rows // TURNED)
        def _(chunk):
            rows = pl.ds(pl.multiple_of(chunk * TURNED, TURNED), TURNED)
            turning[...] = native[k, :, rows, :].astype(F32).reshape(layers * TURNED, LANES)
            for r in range(TURNED):
                values = turning[pl.ds(r, layers, stride=TURNED), :]
                members[k, chunk * TURNED + r] = values.astype(BF16)

    @pl.loop(0, count // 2)
    def _(k):
        turn(k)

    pl.semaphore_wait(barrier, n_dev - 1)
    for pair in range(parts):
        send_tile(0, pair)
    send_source()

    @pl.loop(count // 2, count)
    def _(k):
        turn(k)

    def members_from(k, first):
        return [[members[k + n, first + r] for r in range(PAIR)] for n in range(together)]

    def mix(members_at, vector):
        product = [
            values * vector[r] for member in members_at for r, values in enumerate(member)
        ]
        mixed = jnp.dot(
            spread[...], jnp.concatenate(product, axis=1), preferred_element_type=F32
        )
        pieces = [mixed[:, n * LANES : (n + 1) * LANES] for n in range(len(product))]
        return [pieces[n : n + PAIR] for n in range(0, len(pieces), PAIR)]

    def partial_sum(iteration, origin, pair, store):
        vector = [gathered[iteration, origin, pair * PAIR + r] for r in range(PAIR)]
        first = origin * tile_rows + pair * PAIR

        def sum_of(k):
            values = members_from(k, first)
            mixed = mix(values, vector)
            sums = []
            for r in range(PAIR):
                running = values[0][r].astype(F32) * mixed[0][r]
                for n in range(1, together):
                    running = running + values[n][r].astype(F32) * mixed[n][r]
                sums.append(running)
            return sums

        sums = sum_of(0)
        for k in range(together, count, together):
            sums = [a + b for a, b in zip(sums, sum_of(k))]
        store(sums)

    def owner_cycle(iteration):
        @pl.loop(0, n_dev)
        def _(rank):
            blocks = pl.ds((rank // n_gy) * quads, quads)
            done(f_recv.at[blocks, lax.rem(rank, n_gy)], f_rsem.at[rank])

        source = levels[0][0]
        alpha, ratio = state[0], state[1]

        @pl.loop(0, half_rows // ROWS)
        def _(quad):
            for c in range(n_gy):
                lanes = pl.ds(c * LANES, LANES)
                both = f_recv[quad, c], f_recv[half_blocks * quads + quad, c]
                for r, new in enumerate(unpack_rows(*both)):
                    row = quad * ROWS + r
                    more = new + ratio * f_along[row, :, lanes]
                    f_along[row, :, lanes] = more
                    source[row + 1, :, lanes] = source[row + 1, :, lanes] - alpha * more

        join_halves(source, half_rows)
        result = vcycle(levels, 0, half_rows)

        @pl.when(iteration > 0)
        def _():
            cycle_sent()

        @pl.loop(0, half_rows // ROWS)
        def _(quad):
            for c in range(n_gy):
                lanes = pl.ds(c * LANES, LANES)
                rows = [result[quad * ROWS + r + 1, :, lanes] for r in range(ROWS)]
                b_send[quad, c], b_send[half_blocks * quads + quad, c] = pack_rows(rows)

        @pl.loop(0, n_dev)
        def _(rank):
            blocks = pl.ds((rank // n_gy) * quads, quads)
            send(
                b_send.at[blocks, lax.rem(rank, n_gy)],
                back.at[my_group],
                b_ssem.at[rank],
                b_rsem.at[my_group],
                rank,
            )

    def cycle_sent():
        @pl.loop(0, n_dev)
        def _(rank):
            sent(back.at[0], b_ssem.at[rank], rank)

    def finish(iteration):
        @pl.loop(1, n_dev)
        def _(step):
            rank = lax.rem(me + step, n_dev)
            done(p_recv.at[iteration, rank], p_rsem.at[iteration, rank])
            done(p_recv.at[iteration, rank], p_ssem.at[step])

        sums = jnp.sum(jnp.sum(p_recv[iteration], axis=0), axis=1, keepdims=True)
        norm_next, product = (jnp.broadcast_to(sums[n : n + 1], (1, LANES)) for n in range(2))
        ratio = jnp.where(iteration == 0, 0.0, norm_next / state[2])
        alpha = norm_next / (product - ratio * norm_next / state[0])
        state[0] = alpha
        state[1] = ratio
        state[2] = norm_next
        for n in range(ITERATIONS):
            towards = ratio * blend[2, n] + blend[1, n]
            blend[2, n] = towards
            blend[3, n] = blend[3, n] + alpha * towards
            more = jnp.where(iteration + 1 == n, 1.0, 0.0) + ratio * blend[0, n]
            blend[0, n] = more
            blend[1, n] = blend[1, n] - alpha * more
        for r in range(tile_rows):
            more = image[r] + ratio * along[r]
            along[r] = more
            residual[r] = residual[r] - alpha * more
            cov = cov_res[r] + ratio * cov_dir[r]
            cov_dir[r] = cov
            increment[r] = increment[r] + alpha * cov

    def sum_x(step, pair):
        ens = ens_at(step)
        for hop in range(1, n_gx):
            gx = gx_at(hop)
            arrival = s_recv.at[gx, ens, pair_rows(pair)]
            done(arrival, s_rsem.at[gx, ens, pair])
            for r in range(PAIR):
                row = pair * PAIR + r
                own_sum[ens, row] = own_sum[ens, row] + s_recv[gx, ens, row].astype(F32)

        @pl.when(step > 0)
        def _():
            origin = ens * n_gx + my_gx
            for r in range(PAIR):
                row = pair * PAIR + r
                alpha_fields[0, origin * tile_rows + row] = own_sum[ens, row].astype(BF16)
            remote(
                part_of(origin, pair),
                e_recv.at[my_ens, pair_rows(pair)],
                e_ssem.at[step, pair],
                e_rsem.at[my_ens, pair],
                (ens, my_gx, column),
            )

    @pl.loop(0, ITERATIONS)
    def _(iteration):
        @pl.loop(1, n_ens)
        def _(step):
            receive_and_forward(iteration, step, 0)

        @pl.loop(0, parts * n_blocks)
        def _(job):
            pair = job // n_blocks
            inner = lax.rem(job, n_blocks)
            hop = inner // n_ens
            step = lax.rem(inner, n_ens)
            ens, gx = ens_at(step), gx_at(hop)
            origin = ens * n_gx + gx

            @pl.when((hop == 1) & (step > 0) & (pair < parts - 1))
            def _():
                receive_and_forward(iteration, step, pair + 1)

            @pl.when(hop > 0)
            def _():
                done(tile_of(iteration, origin, pair), r_rsem.at[iteration, origin, pair])

            def store(sums):
                @pl.when(hop == 0)
                def _():
                    for r in range(PAIR):
                        own_sum[ens, pair * PAIR + r] = sums[r]

                @pl.when(hop > 0)
                def _():
                    for r in range(PAIR):
                        alpha_fields[0, origin * tile_rows + pair * PAIR + r] = sums[r].astype(BF16)
                    remote(
                        part_of(origin, pair),
                        s_recv.at[my_gx, ens, pair_rows(pair)],
                        s_ssem.at[step, hop, pair],
                        s_rsem.at[my_gx, ens, pair],
                        (my_ens, gx, column),
                    )

            partial_sum(iteration, origin, pair, store)

            @pl.when((hop == n_gx - 1) & (pair > 0))
            def _():
                sum_x(step, pair - 1)

        @pl.when(iteration > 0)
        def _():
            finish(iteration - 1)

        @pl.when(is_owner)
        def _():
            owner_cycle(iteration)

        tiles_sent(iteration)
        source_sent()

        @pl.loop(0, n_ens)
        def _(step):
            sum_x(lax.rem(step + 1, n_ens), parts - 1)

        @pl.loop(0, groups)
        def _(group):
            done(back.at[group], b_rsem.at[group])

        alpha, ratio = state[0], state[1]
        own = jnp.zeros((1, LANES), F32)
        cross = jnp.zeros((1, LANES), F32)
        cycled = [[] for _ in range(tile_rows)]
        for quad in range(quads):
            for eight in range(eights):
                rows = unpack_rows(back[2 * eight, quad], back[2 * eight + 1, quad])
                for r, row in enumerate(rows):
                    cycled[quad * ROWS + r].append(row)
        cycled = [jnp.concatenate(blocks, axis=0)[:layers] for blocks in cycled]
        sources = []
        for pair in range(parts):
            for step in range(1, n_ens):
                ens = ens_at(step)
                done(e_recv.at[ens, pair_rows(pair)], e_rsem.at[ens, pair])
            for r in range(PAIR):
                row = pair * PAIR + r
                total = own_sum[my_ens, row]
                for step in range(1, n_ens):
                    total = total + e_recv[ens_at(step), row].astype(F32)
                more = total + ratio * ens_along[row]
                ens_along[row] = more
                ens = ens_res[row] - alpha * more
                ens_res[row] = ens
                cov = sea[row : row + 1].astype(F32) * (ens + row_of(scale, row) * cycled[row])
                cov_res[row] = cov
                now = residual[row]
                img = cov + row_of(obs_error, row) * now
                image[row] = img
                masked = sea[row : row + 1].astype(F32) * img
                sources.append(row_of(scale, row) * masked)
                own = own + jnp.sum(now * now, axis=0, keepdims=True)
                cross = cross + jnp.sum(now * img, axis=0, keepdims=True)

                @pl.when(iteration < ITERATIONS - 1)
                def _():
                    gathered[iteration + 1, block, row] = masked.astype(BF16)

            @pl.when(iteration < ITERATIONS - 1)
            def _():
                send_tile(iteration + 1, pair)

        pack_source(sources)
        p_recv[iteration, me, 0:1] = own
        p_recv[iteration, me, 1:2] = cross

        @pl.when(iteration < ITERATIONS - 1)
        def _():
            send_source()

        @pl.loop(1, n_dev)
        def _(step):
            remote(
                p_recv.at[iteration, me],
                p_recv.at[iteration, me],
                p_ssem.at[step],
                p_rsem.at[iteration, me],
                device(lax.rem(me + step, n_dev)),
            )

        sums_sent()

    finish(ITERATIONS - 1)

    @pl.when(is_owner)
    def _():
        cycle_sent()

    @pl.loop(0, n_blocks * parts)
    def _(job):
        origin = job // parts
        pair = lax.rem(job, parts)
        vector = [
            sum(
                blend[3, n] * gathered[n, origin, pair * PAIR + r].astype(F32)
                for n in range(ITERATIONS)
            )
            for r in range(PAIR)
        ]
        first = origin * tile_rows + pair * PAIR
        for k in range(0, count, together):
            at = [[values.astype(F32) for values in member] for member in members_from(k, first)]
            product = [
                (values * vector[r]).astype(BF16) for member in at for r, values in enumerate(member)
            ]
            mixed = jnp.dot(
                spread[...], jnp.concatenate(product, axis=1), preferred_element_type=F32
            )
            for n in range(together):
                for r in range(PAIR):
                    at_lane = (n * PAIR + r) * LANES
                    alpha_fields[k + n, first + r] = mixed[:, at_lane : at_lane + LANES].astype(BF16)


def local(sizes, members, spread, sea_mask, innovations, obs_error, static_scale):
    n_ens, n_gx, n_gy = sizes
    n_blocks = n_ens * n_gx
    n_dev = n_blocks * n_gy
    count, layers, rows, lanes = members.shape
    tile_rows = innovations.shape[1]
    parts = tile_rows // PAIR
    half_rows = rows // 2
    groups = -(-layers // HALF)
    eights = -(-layers // SUB)
    quads = tile_rows // ROWS
    width = lanes * n_gy

    tile = (tile_rows, layers, lanes)
    f_tile = pltpu.VMEM(tile, F32)
    packed = (ROWS * HALF, lanes)
    scratch = [f_tile] * 3 + [
        pltpu.VMEM((count, rows, layers, lanes), BF16),
        pltpu.VMEM((count, layers, rows, lanes), BF16),
        pltpu.VMEM((layers * TURNED, lanes), F32),
        pltpu.VMEM((ITERATIONS, n_blocks, *tile), BF16),
        pltpu.VMEM((n_gx, n_ens, *tile), BF16),
        pltpu.VMEM((n_ens, *tile), BF16),
        pltpu.VMEM((n_ens, *tile), F32),
    ]
    scratch += [f_tile] * 7
    scratch += [
        pltpu.VMEM((half_rows, SUB, width), F32),
        pltpu.VMEM((2 * eights, quads, *packed), BF16),
        pltpu.VMEM((n_blocks * quads, n_gy, *packed), BF16),
        pltpu.VMEM((n_blocks * quads, n_gy, *packed), BF16),
        pltpu.VMEM((2 * eights, quads, *packed), BF16),
        pltpu.VMEM((ITERATIONS, n_dev, 2, lanes), F32),
        pltpu.VMEM((3, 1, lanes), F32),
        pltpu.VMEM((4, ITERATIONS, 1, lanes), F32),
    ]
    for level in range(GRIDS):
        scratch += [pltpu.VMEM((half_rows // 2**level + 2, SUB, width), F32)] * 3
    dma = pltpu.SemaphoreType.DMA
    scratch += [
        dma((groups,)),
        dma((n_dev,)),
        dma((n_dev,)),
        dma((groups,)),
        dma((n_dev,)),
        dma((ITERATIONS, n_dev)),
        dma((n_ens, parts)),
        dma((ITERATIONS, n_blocks, parts)),
        dma((n_ens, n_gx, parts)),
        dma((n_ens, n_gx, parts)),
        dma((n_gx, n_ens, parts)),
        dma((n_ens, parts)),
        dma((n_ens, parts)),
        dma((count,)),
        dma((3, tile_rows)),
    ]
    vmem = pl.BlockSpec(memory_space=pltpu.VMEM)
    hbm = pl.BlockSpec(memory_space=pl.ANY)
    increment, alpha_fields = pl.pallas_call(
        functools.partial(kernel, sizes, groups),
        out_shape=(
            jax.ShapeDtypeStruct(tile, F32),
            jax.ShapeDtypeStruct((count, rows, layers, lanes), BF16),
        ),
        in_specs=[hbm, vmem, vmem, hbm, hbm, hbm],
        out_specs=(vmem, vmem),
        scratch_shapes=scratch,
        compiler_params=pltpu.CompilerParams(
            collective_id=0, has_side_effects=True, vmem_limit_bytes=65000 * 2**10
        ),
        name="window",
    )(members, spread, sea_mask, innovations, obs_error, static_scale)
    return increment.transpose(1, 0, 2), alpha_fields.transpose(0, 2, 1, 3)


def solution(mesh):
    in_specs = (
        P(("ens", "gx"), None, None, "gy"),
        P(),
        P(("ens", "gx"), "gy"),
        P(None, ("ens", "gx"), "gy"),
        P(None, ("ens", "gx"), "gy"),
        P(None, ("ens", "gx"), "gy"),
    )
    out_specs = (P(None, ("ens", "gx"), "gy"), P(("ens", "gx"), None, None, "gy"))
    sizes = tuple(mesh.shape[axis] for axis in ("ens", "gx", "gy"))
    return jax.shard_map(
        functools.partial(local, sizes),
        mesh=mesh,
        in_specs=in_specs,
        out_specs=out_specs,
        check_vma=False,
    )
```

```python
import functools
import math

import jax
import jax.numpy as jnp
from jax import lax
from jax.experimental import pallas as pl
from jax.experimental.pallas import tpu as pltpu
from jax.sharding import PartitionSpec as P

GRIDS = 3
SWEEPS = 2
COARSE_SWEEPS = 4
ITERATIONS = 3
SUB = 8
LANES = 128
PAIR = 2
TURNED = 16
ROWS = 4
HALF = SUB // 2
TOGETHER = 8

diffusivity = 16.0
damping = 0.8
MESH = pl.DeviceIdType.MESH
F32 = jnp.float32
BF16 = jnp.bfloat16


def strength_of(level):
    return diffusivity / 4.0**level


def lane_index(width):
    return lax.broadcasted_iota(jnp.int32, (SUB, width), 1)


def low_half(width):
    return lax.broadcasted_iota(jnp.int32, (SUB, width), 0) < HALF


def swapped(values):
    return pltpu.roll(values, HALF, 0)


def pack_rows(rows):
    low = low_half(LANES)
    firsts = [jnp.where(low, a, swapped(b)) for a, b in (rows[:2], rows[2:])]
    seconds = [jnp.where(low, swapped(a), b) for a, b in (rows[:2], rows[2:])]
    return [jnp.concatenate(blocks, axis=0).astype(BF16) for blocks in (firsts, seconds)]


def unpack_rows(firsts, seconds):
    low = low_half(LANES)
    firsts, seconds = firsts.astype(F32), seconds.astype(F32)
    rows = []
    for at in (0, SUB):
        a, c = firsts[at : at + SUB], seconds[at : at + SUB]
        rows += [jnp.where(low, a, swapped(c)), jnp.where(low, swapped(a), c)]
    return rows


def join_halves(ref, rows):
    low = low_half(ref.shape[-1])
    ref[0] = jnp.where(low, 0.0, swapped(ref[rows]))
    ref[rows + 1] = jnp.where(low, swapped(ref[1]), 0.0)


def over_rows(count, body):
    chunk = min(SUB, count)

    @pl.loop(0, count // chunk)
    def _(block):
        body(block * chunk, chunk)


def beside(here, step):
    width = here.shape[-1]
    lane = lane_index(width)
    left = jnp.where(lane < step, 0.0, pltpu.roll(here, step, 1))
    right = jnp.where(lane >= width - step, 0.0, pltpu.roll(here, width - step, 1))
    return left + right


def around(loaded, index, step):
    return loaded[index] + loaded[index + 2] + beside(loaded[index + 1], step)


def relax(load, source, dst, rows, level, scale=None):
    strength = strength_of(level)
    factor = damping / (1.0 + 4.0 * strength)
    keep = 1.0 - damping
    spread_by = factor * strength
    if scale is not None:
        keep, spread_by = keep * scale, spread_by * scale

    def body(start, chunk):
        loaded = load(start, chunk)
        for r in range(chunk):
            dst[start + r + 1] = (
                keep * loaded[r + 1]
                + factor * source[start + r + 1]
                + spread_by * around(loaded, r, 2**level)
            )

    over_rows(rows, body)
    join_halves(dst, rows)


def rows_of(ref):
    return lambda start, chunk: [ref[start + r] for r in range(chunk + 2)]


def prolonged(ref, coarse):
    def load(start, chunk):
        extra = [coarse[start // 2 + r] for r in range(chunk // 2 + 2)]
        return [ref[start + r] + extra[(r + 1) // 2] for r in range(chunk + 2)]

    return load


def restrict_remainder(src, source, dst, rows, level):
    strength = strength_of(level)
    step = 2**level

    def body(start, chunk):
        loaded = rows_of(src)(start, chunk)
        over = [
            source[start + r + 1]
            - (1.0 + 4.0 * strength) * loaded[r + 1]
            + strength * around(loaded, r, step)
            for r in range(chunk)
        ]
        for r in range(0, chunk, 2):
            both = over[r] + over[r + 1]
            width = both.shape[-1]
            even = lax.rem(lane_index(width) // step, 2) == 0
            other = jnp.where(even, pltpu.roll(both, width - step, 1), pltpu.roll(both, step, 1))
            dst[start // 2 + r // 2 + 1] = 0.25 * (both + other)

    over_rows(rows, body)
    join_halves(dst, rows // 2)


def vcycle(levels, level, rows):
    source, first, second = levels[level]
    factor = damping / (1.0 + 4.0 * strength_of(level))
    relax(rows_of(source), source, first, rows, level, factor)
    before = COARSE_SWEEPS - 2 if level == GRIDS - 1 else SWEEPS - 2
    for _ in range(before):
        relax(rows_of(first), source, second, rows, level)
        first, second = second, first
    if level == GRIDS - 1:
        return first
    restrict_remainder(first, source, levels[level + 1][0], rows, level)
    coarse = vcycle(levels, level + 1, rows // 2)
    load = prolonged(first, coarse)
    for _ in range(SWEEPS):
        relax(load, source, second, rows, level)
        first, second = second, first
        load = rows_of(first)
    return first


def kernel(
    sizes,
    groups,
    members_in,
    spread,
    sea,
    innovations_in,
    obs_error_in,
    scale_in,
    increment,
    alpha_fields,
    innovations,
    obs_error,
    scale,
    members,
    native,
    turning,
    gathered,
    s_recv,
    e_recv,
    own_sum,
    residual,
    along,
    image,
    cov_dir,
    cov_res,
    ens_res,
    ens_along,
    f_along,
    f_send,
    f_recv,
    b_send,
    back,
    p_recv,
    state,
    blend,
    *rest,
):
    n_ens, n_gx, n_gy = sizes
    level_refs = rest[: 3 * GRIDS]
    (f_ssem, f_rsem, b_ssem, b_rsem, p_ssem, p_rsem, r_ssem, r_rsem, s_ssem, s_rsem, e_rsem, m_sem, i_sem) = rest[3 * GRIDS :]
    levels = [level_refs[3 * g : 3 * g + 3] for g in range(GRIDS)]
    n_blocks = n_ens * n_gx
    n_dev = n_blocks * n_gy
    my_ens = lax.axis_index("ens")
    my_gx = lax.axis_index("gx")
    block = my_ens * n_gx + my_gx
    column = lax.axis_index("gy")
    me = block * n_gy + column
    next_group = (me * groups + n_dev - 1) // n_dev
    is_owner = (next_group < groups) & (next_group * n_dev // groups == me)
    my_group = jnp.minimum(next_group, groups - 1)
    layers = spread.shape[0]
    tile_rows = innovations.shape[0]
    count = members.shape[0]
    grid_rows = tile_rows * n_blocks
    half_rows = grid_rows // 2
    half_blocks = n_blocks // 2
    eights = -(-layers // SUB)
    quads = tile_rows // ROWS
    parts = tile_rows // PAIR
    together = math.gcd(count, TOGETHER)

    def row_of(field, row):
        return field[row]

    def device(rank):
        return (rank // (n_gx * n_gy), rank // n_gy % n_gx, rank % n_gy)

    def ens_at(step):
        return lax.rem(my_ens + n_ens - step, n_ens)

    def gx_at(hop):
        return lax.rem(my_gx + hop, n_gx)

    def remote(src, dst, send_sem, recv_sem, target):
        pltpu.make_async_remote_copy(
            src_ref=src,
            dst_ref=dst,
            send_sem=send_sem,
            recv_sem=recv_sem,
            device_id=target,
            device_id_type=MESH,
        ).start()

    def each_other(body):
        def one(blocks_on, columns_on):
            there = lax.rem(block + blocks_on, n_blocks)
            at = lax.rem(column + columns_on, n_gy)
            body((there // n_gx, lax.rem(there, n_gx), at), there * n_gy + at)

        for c in range(1, n_gy):
            one(0, c)

        @pl.loop(1, n_blocks)
        def _(blocks_on):
            for c in range(n_gy):
                one(blocks_on, c)

    def done(ref, sem):
        pltpu.make_async_copy(ref, ref, sem).wait()

    def fetch(k):
        return pltpu.make_async_copy(members_in.at[k], native.at[k], m_sem.at[k])

    fields = [
        pltpu.make_async_copy(given.at[:, r, :], field.at[r], i_sem.at[n, r])
        for n, (given, field) in enumerate(
            ((innovations_in, innovations), (scale_in, scale), (obs_error_in, obs_error))
        )
        for r in range(tile_rows)
    ]
    for copy in fields:
        copy.start()

    @pl.loop(0, count)
    def _(k):
        fetch(k).start()

    barrier = pltpu.get_barrier_semaphore()

    each_other(
        lambda there, rank: pl.semaphore_signal(
            barrier, inc=1, device_id=there, device_id_type=MESH
        )
    )

    def pair_rows(pair):
        return pl.ds(pair * PAIR, PAIR)

    def tile_of(iteration, origin, pair):
        return gathered.at[iteration, origin, pair_rows(pair)]

    def part_of(origin, pair):
        return alpha_fields.at[0, pl.ds(origin * tile_rows + pair * PAIR, PAIR)]

    def forward_x(iteration, step, pair):
        origin = ens_at(step) * n_gx + my_gx
        tile = tile_of(iteration, origin, pair)
        for hop in range(1, n_gx):
            remote(
                tile,
                tile,
                r_ssem,
                r_rsem.at[iteration, origin, pair],
                (my_ens, gx_at(hop), column),
            )

    def receive_and_forward(iteration, step, pair):
        origin = ens_at(step) * n_gx + my_gx
        done(tile_of(iteration, origin, pair), r_rsem.at[iteration, origin, pair])
        forward_x(iteration, step, pair)

    def send_tile(iteration, pair):
        tile = tile_of(iteration, block, pair)
        for step in range(1, n_ens):
            remote(
                tile,
                tile,
                r_ssem,
                r_rsem.at[iteration, block, pair],
                (ens_at(n_ens - step), my_gx, column),
            )
        forward_x(iteration, 0, pair)

    def tiles_sent(sem):
        done(gathered.at[0, pl.ds(0, n_blocks - 1)], sem)

    def pack_source(values):
        for eight in range(eights):
            rows = [value[eight * SUB : (eight + 1) * SUB] for value in values]
            if eight * SUB + SUB > layers:
                tail = jnp.zeros((eight * SUB + SUB - layers, LANES), F32)
                rows = [jnp.concatenate([row, tail], axis=0) for row in rows]
            for quad in range(quads):
                blocks = pack_rows(rows[quad * ROWS : (quad + 1) * ROWS])
                for n, packed in enumerate(blocks):
                    f_send[2 * eight + n, quad] = packed

    def slot(rank):
        return pl.ds(rank * quads, quads)

    def but_own(ref, sem):
        @pl.when(is_owner)
        def _():
            done(ref.at[pl.ds(0, groups - 1)], sem)

        @pl.when(jnp.logical_not(is_owner))
        def _():
            done(ref.at[pl.ds(0, groups)], sem)

    def send_source():
        for group in range(groups):
            rank = group * n_dev // groups

            @pl.when(me != rank)
            def _():
                remote(f_send.at[group], f_recv.at[slot(me)], f_ssem, f_rsem, device(rank))

        @pl.when(is_owner)
        def _():
            for quad in range(quads):
                f_recv[me * quads + quad] = f_send[my_group, quad]

    for copy in fields:
        copy.wait()
    for r in range(tile_rows):
        start = row_of(innovations, r)
        residual[r] = start
        gathered[0, block, r] = (sea[r : r + 1].astype(F32) * start).astype(BF16)
        zero = jnp.zeros_like(start)
        for ref in (along, image, cov_dir, ens_res, ens_along, increment):
            ref[r] = zero
    pack_source([row_of(scale, r) * (sea[r : r + 1].astype(F32) * residual[r]) for r in range(tile_rows)])
    for group in range(groups, 2 * eights):
        back[group] = jnp.zeros(back.shape[1:], BF16)
    blend[...] = jnp.zeros_like(blend)
    blend[1, 0] = jnp.ones((1, LANES), F32)
    state[0] = -jnp.ones((1, LANES), F32)
    state[1] = jnp.zeros((1, LANES), F32)
    state[2] = jnp.ones((1, LANES), F32)

    @pl.when(is_owner)
    def _():
        @pl.loop(0, half_rows)
        def _(row):
            f_along[row] = jnp.zeros(f_along.shape[1:], F32)
            levels[0][0][row + 1] = jnp.zeros(f_along.shape[1:], F32)

    def turn(k):
        fetch(k).wait()

        @pl.loop(0, grid_rows // TURNED)
        def _(chunk):
            rows = pl.ds(pl.multiple_of(chunk * TURNED, TURNED), TURNED)
            turning[...] = native[k, :, rows, :].astype(F32).reshape(layers * TURNED, LANES)
            for r in range(TURNED):
                values = turning[pl.ds(r, layers, stride=TURNED), :]
                members[k, chunk * TURNED + r] = values.astype(BF16)

    @pl.loop(0, count // 2)
    def _(k):
        turn(k)

    pl.semaphore_wait(barrier, n_dev - 1)
    for pair in range(parts):
        send_tile(0, pair)
    send_source()

    @pl.loop(count // 2, count)
    def _(k):
        turn(k)

    def members_from(k, first):
        return [[members[k + n, first + r] for r in range(PAIR)] for n in range(together)]

    def mix(members_at, vector):
        product = [
            values * vector[r] for member in members_at for r, values in enumerate(member)
        ]
        mixed = jnp.dot(
            spread[...], jnp.concatenate(product, axis=1), preferred_element_type=F32
        )
        pieces = [mixed[:, n * LANES : (n + 1) * LANES] for n in range(len(product))]
        return [pieces[n : n + PAIR] for n in range(0, len(pieces), PAIR)]

    def partial_sum(iteration, origin, pair, store):
        vector = [gathered[iteration, origin, pair * PAIR + r] for r in range(PAIR)]
        first = origin * tile_rows + pair * PAIR

        def sum_of(k):
            values = members_from(k, first)
            mixed = mix(values, vector)
            sums = []
            for r in range(PAIR):
                running = values[0][r].astype(F32) * mixed[0][r]
                for n in range(1, together):
                    running = running + values[n][r].astype(F32) * mixed[n][r]
                sums.append(running)
            return sums

        sums = sum_of(0)
        for k in range(together, count, together):
            sums = [a + b for a, b in zip(sums, sum_of(k))]
        store(sums)

    def places(quad, c):
        first = ((quad // quads) * n_gy + c) * quads + lax.rem(quad, quads)
        return first, first + half_blocks * n_gy * quads

    def owner_cycle(iteration):
        done(f_recv.at[pl.ds(0, (n_dev - 1) * quads)], f_rsem)
        source = levels[0][0]
        alpha, ratio = state[0], state[1]

        @pl.loop(0, half_rows // ROWS)
        def _(quad):
            for c in range(n_gy):
                lanes = pl.ds(c * LANES, LANES)
                both = [f_recv[at] for at in places(quad, c)]
                for r, new in enumerate(unpack_rows(*both)):
                    row = quad * ROWS + r
                    more = new + ratio * f_along[row, :, lanes]
                    f_along[row, :, lanes] = more
                    source[row + 1, :, lanes] = source[row + 1, :, lanes] - alpha * more

        join_halves(source, half_rows)
        result = vcycle(levels, 0, half_rows)

        @pl.when(iteration > 0)
        def _():
            cycle_sent()

        @pl.loop(0, half_rows // ROWS)
        def _(quad):
            for c in range(n_gy):
                lanes = pl.ds(c * LANES, LANES)
                rows = [result[quad * ROWS + r + 1, :, lanes] for r in range(ROWS)]
                for at, packed in zip(places(quad, c), pack_rows(rows)):
                    b_send[at] = packed

        each_other(
            lambda there, rank: remote(
                b_send.at[slot(rank)], back.at[my_group], b_ssem, b_rsem, there
            )
        )
        for quad in range(quads):
            back[my_group, quad] = b_send[me * quads + quad]

    def cycle_sent():
        done(b_send.at[pl.ds(0, (n_dev - 1) * quads)], b_ssem)

    def finish(iteration):
        others = p_recv.at[iteration, pl.ds(0, n_dev - 1)]
        done(others, p_rsem.at[iteration])
        done(others, p_ssem)
        sums = jnp.sum(jnp.sum(p_recv[iteration], axis=0), axis=1, keepdims=True)
        norm_next, product = (jnp.broadcast_to(sums[n : n + 1], (1, LANES)) for n in range(2))
        ratio = jnp.where(iteration == 0, 0.0, norm_next / state[2])
        alpha = norm_next / (product - ratio * norm_next / state[0])
        state[0] = alpha
        state[1] = ratio
        state[2] = norm_next
        for n in range(ITERATIONS):
            towards = ratio * blend[2, n] + blend[1, n]
            blend[2, n] = towards
            blend[3, n] = blend[3, n] + alpha * towards
            more = jnp.where(iteration + 1 == n, 1.0, 0.0) + ratio * blend[0, n]
            blend[0, n] = more
            blend[1, n] = blend[1, n] - alpha * more
        for r in range(tile_rows):
            more = image[r] + ratio * along[r]
            along[r] = more
            residual[r] = residual[r] - alpha * more
            cov = cov_res[r] + ratio * cov_dir[r]
            cov_dir[r] = cov
            increment[r] = increment[r] + alpha * cov

    def sum_x(step, pair):
        ens = ens_at(step)
        for hop in range(1, n_gx):
            gx = gx_at(hop)
            arrival = s_recv.at[gx, ens, pair_rows(pair)]
            done(arrival, s_rsem.at[gx, ens, pair])
            for r in range(PAIR):
                row = pair * PAIR + r
                own_sum[ens, row] = own_sum[ens, row] + s_recv[gx, ens, row].astype(F32)

        @pl.when(step > 0)
        def _():
            origin = ens * n_gx + my_gx
            for r in range(PAIR):
                row = pair * PAIR + r
                alpha_fields[0, origin * tile_rows + row] = own_sum[ens, row].astype(BF16)
            remote(
                part_of(origin, pair),
                e_recv.at[my_ens, pair_rows(pair)],
                s_ssem,
                e_rsem.at[my_ens, pair],
                (ens, my_gx, column),
            )

    @pl.loop(0, ITERATIONS)
    def _(iteration):
        @pl.loop(1, n_ens)
        def _(step):
            receive_and_forward(iteration, step, 0)

        @pl.loop(0, parts * n_blocks)
        def _(job):
            @pl.when((job == n_blocks + 0) & (iteration > 0))
            def _():
                finish(iteration - 1)

            @pl.when((job == n_blocks + 0) & is_owner)
            def _():
                owner_cycle(iteration)

            pair = job // n_blocks
            inner = lax.rem(job, n_blocks)
            hop = inner // n_ens
            step = lax.rem(inner, n_ens)
            ens, gx = ens_at(step), gx_at(hop)
            origin = ens * n_gx + gx

            @pl.when((hop == 1) & (step > 0) & (pair < parts - 1))
            def _():
                receive_and_forward(iteration, step, pair + 1)

            @pl.when(hop > 0)
            def _():
                done(tile_of(iteration, origin, pair), r_rsem.at[iteration, origin, pair])

            def store(sums):
                @pl.when(hop == 0)
                def _():
                    for r in range(PAIR):
                        own_sum[ens, pair * PAIR + r] = sums[r]

                @pl.when(hop > 0)
                def _():
                    for r in range(PAIR):
                        alpha_fields[0, origin * tile_rows + pair * PAIR + r] = sums[r].astype(BF16)
                    remote(
                        part_of(origin, pair),
                        s_recv.at[my_gx, ens, pair_rows(pair)],
                        s_ssem,
                        s_rsem.at[my_gx, ens, pair],
                        (my_ens, gx, column),
                    )

            partial_sum(iteration, origin, pair, store)

            @pl.when((hop == n_gx - 1) & (pair > 0))
            def _():
                sum_x(step, pair - 1)

        tiles_sent(r_ssem)
        but_own(f_send, f_ssem)

        @pl.loop(0, n_ens)
        def _(step):
            sum_x(lax.rem(step + 1, n_ens), parts - 1)

        but_own(back, b_rsem)
        alpha, ratio = state[0], state[1]
        own = jnp.zeros((1, LANES), F32)
        cross = jnp.zeros((1, LANES), F32)
        cycled = [[] for _ in range(tile_rows)]
        for quad in range(quads):
            for eight in range(eights):
                rows = unpack_rows(back[2 * eight, quad], back[2 * eight + 1, quad])
                for r, row in enumerate(rows):
                    cycled[quad * ROWS + r].append(row)
        cycled = [jnp.concatenate(blocks, axis=0)[:layers] for blocks in cycled]
        sources = []
        for pair in range(parts):
            for step in range(1, n_ens):
                ens = ens_at(step)
                done(e_recv.at[ens, pair_rows(pair)], e_rsem.at[ens, pair])
            for r in range(PAIR):
                row = pair * PAIR + r
                total = own_sum[my_ens, row]
                for step in range(1, n_ens):
                    total = total + e_recv[ens_at(step), row].astype(F32)
                more = total + ratio * ens_along[row]
                ens_along[row] = more
                ens = ens_res[row] - alpha * more
                ens_res[row] = ens
                cov = sea[row : row + 1].astype(F32) * (ens + row_of(scale, row) * cycled[row])
                cov_res[row] = cov
                now = residual[row]
                img = cov + row_of(obs_error, row) * now
                image[row] = img
                masked = sea[row : row + 1].astype(F32) * img
                sources.append(row_of(scale, row) * masked)
                own = own + jnp.sum(now * now, axis=0, keepdims=True)
                cross = cross + jnp.sum(now * img, axis=0, keepdims=True)

                @pl.when(iteration < ITERATIONS - 1)
                def _():
                    gathered[iteration + 1, block, row] = masked.astype(BF16)

            if pair < parts - 1:

                @pl.when(iteration < ITERATIONS - 1)
                def _():
                    send_tile(iteration + 1, pair)

        pack_source(sources)
        p_recv[iteration, me, 0:1] = own
        p_recv[iteration, me, 1:2] = cross

        @pl.when(iteration < ITERATIONS - 1)
        def _():
            send_source()
            send_tile(iteration + 1, parts - 1)

        mine = p_recv.at[iteration, me]
        each_other(
            lambda there, rank: remote(mine, mine, p_ssem, p_rsem.at[iteration], there)
        )
        tiles_sent(s_ssem)

    finish(ITERATIONS - 1)

    @pl.when(is_owner)
    def _():
        cycle_sent()

    @pl.loop(0, n_blocks * parts)
    def _(job):
        origin = job // parts
        pair = lax.rem(job, parts)
        vector = [
            sum(
                blend[3, n] * gathered[n, origin, pair * PAIR + r].astype(F32)
                for n in range(ITERATIONS)
            )
            for r in range(PAIR)
        ]
        first = origin * tile_rows + pair * PAIR
        for k in range(0, count, together):
            at = [[values.astype(F32) for values in member] for member in members_from(k, first)]
            product = [
                (values * vector[r]).astype(BF16) for member in at for r, values in enumerate(member)
            ]
            mixed = jnp.dot(
                spread[...], jnp.concatenate(product, axis=1), preferred_element_type=F32
            )
            for n in range(together):
                for r in range(PAIR):
                    at_lane = (n * PAIR + r) * LANES
                    alpha_fields[k + n, first + r] = mixed[:, at_lane : at_lane + LANES].astype(BF16)


def local(sizes, members, spread, sea_mask, innovations, obs_error, static_scale):
    n_ens, n_gx, n_gy = sizes
    n_blocks = n_ens * n_gx
    n_dev = n_blocks * n_gy
    count, layers, rows, lanes = members.shape
    tile_rows = innovations.shape[1]
    parts = tile_rows // PAIR
    half_rows = rows // 2
    groups = -(-layers // HALF)
    eights = -(-layers // SUB)
    quads = tile_rows // ROWS
    width = lanes * n_gy

    tile = (tile_rows, layers, lanes)
    f_tile = pltpu.VMEM(tile, F32)
    packed = (ROWS * HALF, lanes)
    scratch = [f_tile] * 3 + [
        pltpu.VMEM((count, rows, layers, lanes), BF16),
        pltpu.VMEM((count, layers, rows, lanes), BF16),
        pltpu.VMEM((layers * TURNED, lanes), F32),
        pltpu.VMEM((ITERATIONS, n_blocks, *tile), BF16),
        pltpu.VMEM((n_gx, n_ens, *tile), BF16),
        pltpu.VMEM((n_ens, *tile), BF16),
        pltpu.VMEM((n_ens, *tile), F32),
    ]
    scratch += [f_tile] * 7
    scratch += [
        pltpu.VMEM((half_rows, SUB, width), F32),
        pltpu.VMEM((2 * eights, quads, *packed), BF16),
        pltpu.VMEM((n_dev * quads, *packed), BF16),
        pltpu.VMEM((n_dev * quads, *packed), BF16),
        pltpu.VMEM((2 * eights, quads, *packed), BF16),
        pltpu.VMEM((ITERATIONS, n_dev, 2, lanes), F32),
        pltpu.VMEM((3, 1, lanes), F32),
        pltpu.VMEM((4, ITERATIONS, 1, lanes), F32),
    ]
    for level in range(GRIDS):
        scratch += [pltpu.VMEM((half_rows // 2**level + 2, SUB, width), F32)] * 3
    dma = pltpu.SemaphoreType.DMA
    scratch += [
        dma(()),
        dma(()),
        dma(()),
        dma(()),
        dma(()),
        dma((ITERATIONS,)),
        dma(()),
        dma((ITERATIONS, n_blocks, parts)),
        dma(()),
        dma((n_gx, n_ens, parts)),
        dma((n_ens, parts)),
        dma((count,)),
        dma((3, tile_rows)),
    ]
    vmem = pl.BlockSpec(memory_space=pltpu.VMEM)
    hbm = pl.BlockSpec(memory_space=pl.ANY)
    increment, alpha_fields = pl.pallas_call(
        functools.partial(kernel, sizes, groups),
        out_shape=(
            jax.ShapeDtypeStruct(tile, F32),
            jax.ShapeDtypeStruct((count, rows, layers, lanes), BF16),
        ),
        in_specs=[hbm, vmem, vmem, hbm, hbm, hbm],
        out_specs=(vmem, vmem),
        scratch_shapes=scratch,
        compiler_params=pltpu.CompilerParams(
            collective_id=0, has_side_effects=True, vmem_limit_bytes=65000 * 2**10
        ),
        name="window",
    )(members, spread, sea_mask, innovations, obs_error, static_scale)
    return increment.transpose(1, 0, 2), alpha_fields.transpose(0, 2, 1, 3)


def solution(mesh):
    in_specs = (
        P(("ens", "gx"), None, None, "gy"),
        P(),
        P(("ens", "gx"), "gy"),
        P(None, ("ens", "gx"), "gy"),
        P(None, ("ens", "gx"), "gy"),
        P(None, ("ens", "gx"), "gy"),
    )
    out_specs = (P(None, ("ens", "gx"), "gy"), P(("ens", "gx"), None, None, "gy"))
    sizes = tuple(mesh.shape[axis] for axis in ("ens", "gx", "gy"))
    return jax.shard_map(
        functools.partial(local, sizes),
        mesh=mesh,
        in_specs=in_specs,
        out_specs=out_specs,
        check_vma=False,
    )
```

```python
import functools
import math

import jax
import jax.numpy as jnp
from jax import lax
from jax.experimental import pallas as pl
from jax.experimental.pallas import tpu as pltpu
from jax.sharding import PartitionSpec as P

GRIDS = 3
SWEEPS = 2
COARSE_SWEEPS = 4
ITERATIONS = 3
SUB = 8
LANES = 128
PAIR = 2
TURNED = 16
ROWS = 4
HALF = SUB // 2
TOGETHER = 8

diffusivity = 16.0
damping = 0.8
MESH = pl.DeviceIdType.MESH
F32 = jnp.float32
BF16 = jnp.bfloat16


def strength_of(level):
    return diffusivity / 4.0**level


def lane_index(width):
    return lax.broadcasted_iota(jnp.int32, (SUB, width), 1)


def low_half(width):
    return lax.broadcasted_iota(jnp.int32, (SUB, width), 0) < HALF


def swapped(values):
    return pltpu.roll(values, HALF, 0)


def pack_rows(rows):
    low = low_half(LANES)
    firsts = [jnp.where(low, a, swapped(b)) for a, b in (rows[:2], rows[2:])]
    seconds = [jnp.where(low, swapped(a), b) for a, b in (rows[:2], rows[2:])]
    return [jnp.concatenate(blocks, axis=0).astype(BF16) for blocks in (firsts, seconds)]


def unpack_rows(firsts, seconds):
    low = low_half(LANES)
    firsts, seconds = firsts.astype(F32), seconds.astype(F32)
    rows = []
    for at in (0, SUB):
        a, c = firsts[at : at + SUB], seconds[at : at + SUB]
        rows += [jnp.where(low, a, swapped(c)), jnp.where(low, swapped(a), c)]
    return rows


def join_halves(ref, rows):
    low = low_half(ref.shape[-1])
    ref[0] = jnp.where(low, 0.0, swapped(ref[rows]))
    ref[rows + 1] = jnp.where(low, swapped(ref[1]), 0.0)


def over_rows(count, body):
    chunk = min(SUB, count)

    @pl.loop(0, count // chunk)
    def _(block):
        body(block * chunk, chunk)


def beside(here, step):
    width = here.shape[-1]
    lane = lane_index(width)
    left = jnp.where(lane < step, 0.0, pltpu.roll(here, step, 1))
    right = jnp.where(lane >= width - step, 0.0, pltpu.roll(here, width - step, 1))
    return left + right


def around(loaded, index, step):
    return loaded[index] + loaded[index + 2] + beside(loaded[index + 1], step)


def relax(load, source, dst, rows, level, scale=None):
    strength = strength_of(level)
    factor = damping / (1.0 + 4.0 * strength)
    keep = 1.0 - damping
    spread_by = factor * strength
    if scale is not None:
        keep, spread_by = keep * scale, spread_by * scale

    def body(start, chunk):
        loaded = load(start, chunk)
        for r in range(chunk):
            dst[start + r + 1] = (
                keep * loaded[r + 1]
                + factor * source[start + r + 1]
                + spread_by * around(loaded, r, 2**level)
            )

    over_rows(rows, body)
    join_halves(dst, rows)


def rows_of(ref):
    return lambda start, chunk: [ref[start + r] for r in range(chunk + 2)]


def prolonged(ref, coarse):
    def load(start, chunk):
        extra = [coarse[start // 2 + r] for r in range(chunk // 2 + 2)]
        return [ref[start + r] + extra[(r + 1) // 2] for r in range(chunk + 2)]

    return load


def restrict_remainder(src, source, dst, rows, level):
    strength = strength_of(level)
    step = 2**level

    def body(start, chunk):
        loaded = rows_of(src)(start, chunk)
        over = [
            source[start + r + 1]
            - (1.0 + 4.0 * strength) * loaded[r + 1]
            + strength * around(loaded, r, step)
            for r in range(chunk)
        ]
        for r in range(0, chunk, 2):
            both = over[r] + over[r + 1]
            width = both.shape[-1]
            even = lax.rem(lane_index(width) // step, 2) == 0
            other = jnp.where(even, pltpu.roll(both, width - step, 1), pltpu.roll(both, step, 1))
            dst[start // 2 + r // 2 + 1] = 0.25 * (both + other)

    over_rows(rows, body)
    join_halves(dst, rows // 2)


def vcycle(levels, level, rows):
    source, first, second = levels[level]
    factor = damping / (1.0 + 4.0 * strength_of(level))
    relax(rows_of(source), source, first, rows, level, factor)
    before = COARSE_SWEEPS - 2 if level == GRIDS - 1 else SWEEPS - 2
    for _ in range(before):
        relax(rows_of(first), source, second, rows, level)
        first, second = second, first
    if level == GRIDS - 1:
        return first
    restrict_remainder(first, source, levels[level + 1][0], rows, level)
    coarse = vcycle(levels, level + 1, rows // 2)
    load = prolonged(first, coarse)
    for _ in range(SWEEPS):
        relax(load, source, second, rows, level)
        first, second = second, first
        load = rows_of(first)
    return first


def kernel(
    sizes,
    groups,
    members_in,
    spread,
    sea,
    innovations_in,
    obs_error_in,
    scale_in,
    increment,
    weights,
    turned,
    staged,
    innovations,
    obs_error,
    scale,
    members,
    native,
    turning,
    gathered,
    s_recv,
    e_recv,
    own_sum,
    residual,
    along,
    image,
    cov_dir,
    cov_res,
    ens_res,
    ens_along,
    f_along,
    f_send,
    f_recv,
    b_send,
    back,
    p_recv,
    state,
    blend,
    *rest,
):
    n_ens, n_gx, n_gy = sizes
    level_refs = rest[: 3 * GRIDS]
    (f_ssem, f_rsem, b_ssem, b_rsem, p_ssem, p_rsem, r_ssem, r_rsem, s_ssem, s_rsem, e_rsem, m_sem, i_sem, t_sem, w_sem) = rest[3 * GRIDS :]
    levels = [level_refs[3 * g : 3 * g + 3] for g in range(GRIDS)]
    n_blocks = n_ens * n_gx
    n_dev = n_blocks * n_gy
    my_ens = lax.axis_index("ens")
    my_gx = lax.axis_index("gx")
    block = my_ens * n_gx + my_gx
    column = lax.axis_index("gy")
    me = block * n_gy + column
    next_group = (me * groups + n_dev - 1) // n_dev
    is_owner = (next_group < groups) & (next_group * n_dev // groups == me)
    my_group = jnp.minimum(next_group, groups - 1)
    layers = spread.shape[0]
    tile_rows = innovations.shape[0]
    count = members.shape[0]
    grid_rows = tile_rows * n_blocks
    half_rows = grid_rows // 2
    half_blocks = n_blocks // 2
    eights = -(-layers // SUB)
    quads = tile_rows // ROWS
    parts = tile_rows // PAIR
    together = math.gcd(count, TOGETHER)

    def row_of(field, row):
        return field[row]

    def device(rank):
        return (rank // (n_gx * n_gy), rank // n_gy % n_gx, rank % n_gy)

    def ens_at(step):
        return lax.rem(my_ens + n_ens - step, n_ens)

    def gx_at(hop):
        return lax.rem(my_gx + hop, n_gx)

    def remote(src, dst, send_sem, recv_sem, target):
        pltpu.make_async_remote_copy(
            src_ref=src,
            dst_ref=dst,
            send_sem=send_sem,
            recv_sem=recv_sem,
            device_id=target,
            device_id_type=MESH,
        ).start()

    def each_other(body):
        def one(blocks_on, columns_on):
            there = lax.rem(block + blocks_on, n_blocks)
            at = lax.rem(column + columns_on, n_gy)
            body((there // n_gx, lax.rem(there, n_gx), at), there * n_gy + at)

        for c in range(1, n_gy):
            one(0, c)

        @pl.loop(1, n_blocks)
        def _(blocks_on):
            for c in range(n_gy):
                one(blocks_on, c)

    def done(ref, sem):
        pltpu.make_async_copy(ref, ref, sem).wait()

    def fetch(k):
        return pltpu.make_async_copy(members_in.at[k], native.at[k], m_sem.at[k])

    fields = [
        pltpu.make_async_copy(given.at[:, r, :], field.at[r], i_sem.at[n, r])
        for n, (given, field) in enumerate(
            ((innovations_in, innovations), (scale_in, scale), (obs_error_in, obs_error))
        )
        for r in range(tile_rows)
    ]
    for copy in fields:
        copy.start()

    @pl.loop(0, count)
    def _(k):
        fetch(k).start()

    barrier = pltpu.get_barrier_semaphore()

    each_other(
        lambda there, rank: pl.semaphore_signal(
            barrier, inc=1, device_id=there, device_id_type=MESH
        )
    )

    def pair_rows(pair):
        return pl.ds(pair * PAIR, PAIR)

    def tile_of(iteration, origin, pair):
        return gathered.at[iteration, origin, pair_rows(pair)]

    def part_of(origin, pair):
        return staged.at[pl.ds(origin * tile_rows + pair * PAIR, PAIR)]

    def forward_x(iteration, step, pair):
        origin = ens_at(step) * n_gx + my_gx
        tile = tile_of(iteration, origin, pair)
        for hop in range(1, n_gx):
            remote(
                tile,
                tile,
                r_ssem,
                r_rsem.at[iteration, origin, pair],
                (my_ens, gx_at(hop), column),
            )

    def receive_and_forward(iteration, step, pair):
        origin = ens_at(step) * n_gx + my_gx
        done(tile_of(iteration, origin, pair), r_rsem.at[iteration, origin, pair])
        forward_x(iteration, step, pair)

    def send_tile(iteration, pair):
        tile = tile_of(iteration, block, pair)
        for step in range(1, n_ens):
            remote(
                tile,
                tile,
                r_ssem,
                r_rsem.at[iteration, block, pair],
                (ens_at(n_ens - step), my_gx, column),
            )
        forward_x(iteration, 0, pair)

    def tiles_sent(sem):
        done(gathered.at[0, pl.ds(0, n_blocks - 1)], sem)

    def pack_source(values):
        for eight in range(eights):
            rows = [value[eight * SUB : (eight + 1) * SUB] for value in values]
            if eight * SUB + SUB > layers:
                tail = jnp.zeros((eight * SUB + SUB - layers, LANES), F32)
                rows = [jnp.concatenate([row, tail], axis=0) for row in rows]
            for quad in range(quads):
                blocks = pack_rows(rows[quad * ROWS : (quad + 1) * ROWS])
                for n, packed in enumerate(blocks):
                    f_send[2 * eight + n, quad] = packed

    def slot(rank):
        return pl.ds(rank * quads, quads)

    def but_own(ref, sem):
        @pl.when(is_owner)
        def _():
            done(ref.at[pl.ds(0, groups - 1)], sem)

        @pl.when(jnp.logical_not(is_owner))
        def _():
            done(ref.at[pl.ds(0, groups)], sem)

    def send_source():
        for group in range(groups):
            rank = group * n_dev // groups

            @pl.when(me != rank)
            def _():
                remote(f_send.at[group], f_recv.at[slot(me)], f_ssem, f_rsem, device(rank))

        @pl.when(is_owner)
        def _():
            for quad in range(quads):
                f_recv[me * quads + quad] = f_send[my_group, quad]

    for copy in fields:
        copy.wait()
    for r in range(tile_rows):
        start = row_of(innovations, r)
        residual[r] = start
        gathered[0, block, r] = (sea[r : r + 1].astype(F32) * start).astype(BF16)
        zero = jnp.zeros_like(start)
        for ref in (along, image, cov_dir, ens_res, ens_along, increment):
            ref[r] = zero
    pack_source([row_of(scale, r) * (sea[r : r + 1].astype(F32) * residual[r]) for r in range(tile_rows)])
    for group in range(groups, 2 * eights):
        back[group] = jnp.zeros(back.shape[1:], BF16)
    blend[...] = jnp.zeros_like(blend)
    blend[1, 0] = jnp.ones((1, LANES), F32)
    state[0] = -jnp.ones((1, LANES), F32)
    state[1] = jnp.zeros((1, LANES), F32)
    state[2] = jnp.ones((1, LANES), F32)

    @pl.when(is_owner)
    def _():
        @pl.loop(0, half_rows)
        def _(row):
            f_along[row] = jnp.zeros(f_along.shape[1:], F32)
            levels[0][0][row + 1] = jnp.zeros(f_along.shape[1:], F32)

    def keep(k):
        return pltpu.make_async_copy(members.at[k], turned.at[k], t_sem.at[k])

    def turn(k):
        fetch(k).wait()

        @pl.loop(0, grid_rows // TURNED)
        def _(chunk):
            rows = pl.ds(pl.multiple_of(chunk * TURNED, TURNED), TURNED)
            turning[...] = native[k, :, rows, :].astype(F32).reshape(layers * TURNED, LANES)
            for r in range(TURNED):
                values = turning[pl.ds(r, layers, stride=TURNED), :]
                members[k, chunk * TURNED + r] = values.astype(BF16)

        keep(k).start()

    @pl.loop(0, count // 2)
    def _(k):
        turn(k)

    pl.semaphore_wait(barrier, n_dev - 1)
    for pair in range(parts):
        send_tile(0, pair)
    send_source()

    @pl.loop(count // 2, count)
    def _(k):
        turn(k)

    def members_from(k, first):
        return [[members[k + n, first + r] for r in range(PAIR)] for n in range(together)]

    def mix(members_at, vector):
        product = [
            values * vector[r] for member in members_at for r, values in enumerate(member)
        ]
        mixed = jnp.dot(
            spread[...], jnp.concatenate(product, axis=1), preferred_element_type=F32
        )
        pieces = [mixed[:, n * LANES : (n + 1) * LANES] for n in range(len(product))]
        return [pieces[n : n + PAIR] for n in range(0, len(pieces), PAIR)]

    def partial_sum(iteration, origin, pair, store):
        vector = [gathered[iteration, origin, pair * PAIR + r] for r in range(PAIR)]
        first = origin * tile_rows + pair * PAIR

        def sum_of(k):
            values = members_from(k, first)
            mixed = mix(values, vector)
            sums = []
            for r in range(PAIR):
                running = values[0][r].astype(F32) * mixed[0][r]
                for n in range(1, together):
                    running = running + values[n][r].astype(F32) * mixed[n][r]
                sums.append(running)
            return sums

        sums = sum_of(0)
        for k in range(together, count, together):
            sums = [a + b for a, b in zip(sums, sum_of(k))]
        store(sums)

    def places(quad, c):
        first = ((quad // quads) * n_gy + c) * quads + lax.rem(quad, quads)
        return first, first + half_blocks * n_gy * quads

    def owner_cycle(iteration):
        done(f_recv.at[pl.ds(0, (n_dev - 1) * quads)], f_rsem)
        source = levels[0][0]
        alpha, ratio = state[0], state[1]

        @pl.loop(0, half_rows // ROWS)
        def _(quad):
            for c in range(n_gy):
                lanes = pl.ds(c * LANES, LANES)
                both = [f_recv[at] for at in places(quad, c)]
                for r, new in enumerate(unpack_rows(*both)):
                    row = quad * ROWS + r
                    more = new + ratio * f_along[row, :, lanes]
                    f_along[row, :, lanes] = more
                    source[row + 1, :, lanes] = source[row + 1, :, lanes] - alpha * more

        join_halves(source, half_rows)
        result = vcycle(levels, 0, half_rows)

        @pl.when(iteration > 0)
        def _():
            cycle_sent()

        @pl.loop(0, half_rows // ROWS)
        def _(quad):
            for c in range(n_gy):
                lanes = pl.ds(c * LANES, LANES)
                rows = [result[quad * ROWS + r + 1, :, lanes] for r in range(ROWS)]
                for at, packed in zip(places(quad, c), pack_rows(rows)):
                    b_send[at] = packed

        each_other(
            lambda there, rank: remote(
                b_send.at[slot(rank)], back.at[my_group], b_ssem, b_rsem, there
            )
        )
        for quad in range(quads):
            back[my_group, quad] = b_send[me * quads + quad]

    def cycle_sent():
        done(b_send.at[pl.ds(0, (n_dev - 1) * quads)], b_ssem)

    def finish(iteration):
        others = p_recv.at[iteration, pl.ds(0, n_dev - 1)]
        done(others, p_rsem.at[iteration])
        done(others, p_ssem)
        sums = jnp.sum(jnp.sum(p_recv[iteration], axis=0), axis=1, keepdims=True)
        norm_next, product = (jnp.broadcast_to(sums[n : n + 1], (1, LANES)) for n in range(2))
        ratio = jnp.where(iteration == 0, 0.0, norm_next / state[2])
        alpha = norm_next / (product - ratio * norm_next / state[0])
        state[0] = alpha
        state[1] = ratio
        state[2] = norm_next
        for n in range(ITERATIONS):
            towards = ratio * blend[2, n] + blend[1, n]
            blend[2, n] = towards
            blend[3, n] = blend[3, n] + alpha * towards
            more = jnp.where(iteration + 1 == n, 1.0, 0.0) + ratio * blend[0, n]
            blend[0, n] = more
            blend[1, n] = blend[1, n] - alpha * more
        for r in range(tile_rows):
            more = image[r] + ratio * along[r]
            along[r] = more
            residual[r] = residual[r] - alpha * more
            cov = cov_res[r] + ratio * cov_dir[r]
            cov_dir[r] = cov
            increment[r] = increment[r] + alpha * cov

    def sum_x(step, pair):
        ens = ens_at(step)
        for hop in range(1, n_gx):
            gx = gx_at(hop)
            arrival = s_recv.at[gx, ens, pair_rows(pair)]
            done(arrival, s_rsem.at[gx, ens, pair])
            for r in range(PAIR):
                row = pair * PAIR + r
                own_sum[ens, row] = own_sum[ens, row] + s_recv[gx, ens, row].astype(F32)

        @pl.when(step > 0)
        def _():
            origin = ens * n_gx + my_gx
            for r in range(PAIR):
                row = pair * PAIR + r
                staged[origin * tile_rows + row] = own_sum[ens, row].astype(BF16)
            remote(
                part_of(origin, pair),
                e_recv.at[my_ens, pair_rows(pair)],
                s_ssem,
                e_rsem.at[my_ens, pair],
                (ens, my_gx, column),
            )

    @pl.loop(0, ITERATIONS)
    def _(iteration):
        @pl.loop(1, n_ens)
        def _(step):
            receive_and_forward(iteration, step, 0)

        @pl.loop(0, parts * n_blocks)
        def _(job):
            @pl.when((job == n_blocks + 0) & (iteration > 0))
            def _():
                finish(iteration - 1)

            @pl.when((job == n_blocks + 0) & is_owner)
            def _():
                owner_cycle(iteration)

            pair = job // n_blocks
            inner = lax.rem(job, n_blocks)
            hop = inner // n_ens
            step = lax.rem(inner, n_ens)
            ens, gx = ens_at(step), gx_at(hop)
            origin = ens * n_gx + gx

            @pl.when((hop == 1) & (step > 0) & (pair < parts - 1))
            def _():
                receive_and_forward(iteration, step, pair + 1)

            @pl.when(hop > 0)
            def _():
                done(tile_of(iteration, origin, pair), r_rsem.at[iteration, origin, pair])

            def store(sums):
                @pl.when(hop == 0)
                def _():
                    for r in range(PAIR):
                        own_sum[ens, pair * PAIR + r] = sums[r]

                @pl.when(hop > 0)
                def _():
                    for r in range(PAIR):
                        staged[origin * tile_rows + pair * PAIR + r] = sums[r].astype(BF16)
                    remote(
                        part_of(origin, pair),
                        s_recv.at[my_gx, ens, pair_rows(pair)],
                        s_ssem,
                        s_rsem.at[my_gx, ens, pair],
                        (my_ens, gx, column),
                    )

            partial_sum(iteration, origin, pair, store)

            @pl.when((hop == n_gx - 1) & (pair > 0))
            def _():
                sum_x(step, pair - 1)

        tiles_sent(r_ssem)
        but_own(f_send, f_ssem)

        @pl.loop(0, n_ens)
        def _(step):
            sum_x(lax.rem(step + 1, n_ens), parts - 1)

        but_own(back, b_rsem)
        alpha, ratio = state[0], state[1]
        own = jnp.zeros((1, LANES), F32)
        cross = jnp.zeros((1, LANES), F32)
        cycled = [[] for _ in range(tile_rows)]
        for quad in range(quads):
            for eight in range(eights):
                rows = unpack_rows(back[2 * eight, quad], back[2 * eight + 1, quad])
                for r, row in enumerate(rows):
                    cycled[quad * ROWS + r].append(row)
        cycled = [jnp.concatenate(blocks, axis=0)[:layers] for blocks in cycled]
        sources = []
        for pair in range(parts):
            for step in range(1, n_ens):
                ens = ens_at(step)
                done(e_recv.at[ens, pair_rows(pair)], e_rsem.at[ens, pair])
            for r in range(PAIR):
                row = pair * PAIR + r
                total = own_sum[my_ens, row]
                for step in range(1, n_ens):
                    total = total + e_recv[ens_at(step), row].astype(F32)
                more = total + ratio * ens_along[row]
                ens_along[row] = more
                ens = ens_res[row] - alpha * more
                ens_res[row] = ens
                cov = sea[row : row + 1].astype(F32) * (ens + row_of(scale, row) * cycled[row])
                cov_res[row] = cov
                now = residual[row]
                img = cov + row_of(obs_error, row) * now
                image[row] = img
                masked = sea[row : row + 1].astype(F32) * img
                sources.append(row_of(scale, row) * masked)
                own = own + jnp.sum(now * now, axis=0, keepdims=True)
                cross = cross + jnp.sum(now * img, axis=0, keepdims=True)

                @pl.when(iteration < ITERATIONS - 1)
                def _():
                    gathered[iteration + 1, block, row] = masked.astype(BF16)

            if pair < parts - 1:

                @pl.when(iteration < ITERATIONS - 1)
                def _():
                    send_tile(iteration + 1, pair)

        pack_source(sources)
        p_recv[iteration, me, 0:1] = own
        p_recv[iteration, me, 1:2] = cross

        @pl.when(iteration < ITERATIONS - 1)
        def _():
            send_source()
            send_tile(iteration + 1, parts - 1)

        mine = p_recv.at[iteration, me]
        each_other(
            lambda there, rank: remote(mine, mine, p_ssem, p_rsem.at[iteration], there)
        )
        tiles_sent(s_ssem)

    finish(ITERATIONS - 1)

    @pl.when(is_owner)
    def _():
        cycle_sent()

    def give(origin):
        return pltpu.make_async_copy(
            own_sum.at[lax.rem(origin, n_ens)],
            weights.at[pl.ds(origin * tile_rows, tile_rows)],
            w_sem.at[lax.rem(origin, n_ens)],
        )

    @pl.loop(0, n_blocks)
    def _(origin):
        held = lax.rem(origin, n_ens)

        @pl.when(origin >= n_ens)
        def _():
            give(origin - n_ens).wait()

        for r in range(tile_rows):
            own_sum[held, r] = sum(
                blend[3, n] * gathered[n, origin, r].astype(F32) for n in range(ITERATIONS)
            )
        give(origin).start()

    @pl.loop(n_blocks - n_ens, n_blocks)
    def _(origin):
        give(origin).wait()

    @pl.loop(0, count)
    def _(k):
        keep(k).wait()


def fields_kernel(members, spread, weights, increment, alpha_fields, increment_out, turning, sem):
    layers = spread.shape[0]
    rows = members.shape[1]
    copies = [
        pltpu.make_async_copy(increment.at[r], increment_out.at[:, r, :], sem.at[r])
        for r in range(increment.shape[0])
    ]

    @pl.when(pl.program_id(0) == 0)
    def _():
        for copy in copies:
            copy.start()

    buffers = turning.shape[0]

    @pl.loop(0, rows // (TURNED * buffers))
    def _(chunk):
        for n in range(buffers):
            first = pl.multiple_of((chunk * buffers + n) * TURNED, TURNED)
            product = [
                (members[0, first + r].astype(F32) * weights[first + r]).astype(BF16)
                for r in range(TURNED)
            ]
            mixed = jnp.dot(
                spread[...], jnp.concatenate(product, axis=1), preferred_element_type=F32
            )
            for r in range(TURNED):
                turning[n, pl.ds(r, layers, stride=TURNED), :] = mixed[:, r * LANES : (r + 1) * LANES]
            alpha_fields[0, :, pl.ds(first, TURNED), :] = (
                turning[n].reshape(layers, TURNED, LANES).astype(BF16)
            )

    @pl.when(pl.program_id(0) == pl.num_programs(0) - 1)
    def _():
        for copy in copies:
            copy.wait()


def local(sizes, members, spread, sea_mask, innovations, obs_error, static_scale):
    n_ens, n_gx, n_gy = sizes
    n_blocks = n_ens * n_gx
    n_dev = n_blocks * n_gy
    count, layers, rows, lanes = members.shape
    tile_rows = innovations.shape[1]
    parts = tile_rows // PAIR
    half_rows = rows // 2
    groups = -(-layers // HALF)
    eights = -(-layers // SUB)
    quads = tile_rows // ROWS
    width = lanes * n_gy

    tile = (tile_rows, layers, lanes)
    f_tile = pltpu.VMEM(tile, F32)
    packed = (ROWS * HALF, lanes)
    scratch = [pltpu.VMEM((rows, layers, lanes), BF16)] + [f_tile] * 3 + [
        pltpu.VMEM((count, rows, layers, lanes), BF16),
        pltpu.VMEM((count, layers, rows, lanes), BF16),
        pltpu.VMEM((layers * TURNED, lanes), F32),
        pltpu.VMEM((ITERATIONS, n_blocks, *tile), BF16),
        pltpu.VMEM((n_gx, n_ens, *tile), BF16),
        pltpu.VMEM((n_ens, *tile), BF16),
        pltpu.VMEM((n_ens, *tile), F32),
    ]
    scratch += [f_tile] * 7
    scratch += [
        pltpu.VMEM((half_rows, SUB, width), F32),
        pltpu.VMEM((2 * eights, quads, *packed), BF16),
        pltpu.VMEM((n_dev * quads, *packed), BF16),
        pltpu.VMEM((n_dev * quads, *packed), BF16),
        pltpu.VMEM((2 * eights, quads, *packed), BF16),
        pltpu.VMEM((ITERATIONS, n_dev, 2, lanes), F32),
        pltpu.VMEM((3, 1, lanes), F32),
        pltpu.VMEM((4, ITERATIONS, 1, lanes), F32),
    ]
    for level in range(GRIDS):
        scratch += [pltpu.VMEM((half_rows // 2**level + 2, SUB, width), F32)] * 3
    dma = pltpu.SemaphoreType.DMA
    scratch += [
        dma(()),
        dma(()),
        dma(()),
        dma(()),
        dma(()),
        dma((ITERATIONS,)),
        dma(()),
        dma((ITERATIONS, n_blocks, parts)),
        dma(()),
        dma((n_gx, n_ens, parts)),
        dma((n_ens, parts)),
        dma((count,)),
        dma((3, tile_rows)),
        dma((count,)),
        dma((n_ens,)),
    ]
    vmem = pl.BlockSpec(memory_space=pltpu.VMEM)
    hbm = pl.BlockSpec(memory_space=pl.ANY)
    increment, weights, turned = pl.pallas_call(
        functools.partial(kernel, sizes, groups),
        out_shape=(
            jax.ShapeDtypeStruct(tile, F32),
            jax.ShapeDtypeStruct((rows, layers, lanes), F32),
            jax.ShapeDtypeStruct((count, rows, layers, lanes), BF16),
        ),
        in_specs=[hbm, vmem, vmem, hbm, hbm, hbm],
        out_specs=(vmem, hbm, hbm),
        scratch_shapes=scratch,
        compiler_params=pltpu.CompilerParams(
            collective_id=0, has_side_effects=True, vmem_limit_bytes=65000 * 2**10
        ),
        name="window",
    )(members, spread, sea_mask, innovations, obs_error, static_scale)
    buffers = math.gcd(rows // TURNED, 2)

    def whole(shape):
        return pl.BlockSpec(shape, lambda k: (0,) * len(shape))

    alpha_fields, increment = pl.pallas_call(
        fields_kernel,
        grid=(count,),
        out_shape=(
            jax.ShapeDtypeStruct((count, layers, rows, lanes), BF16),
            jax.ShapeDtypeStruct((layers, tile_rows, lanes), F32),
        ),
        in_specs=[
            pl.BlockSpec((1, rows, layers, lanes), lambda k: (k, 0, 0, 0)),
            whole((layers, layers)),
            whole((rows, layers, lanes)),
            whole(tile),
        ],
        out_specs=(pl.BlockSpec((1, layers, rows, lanes), lambda k: (k, 0, 0, 0)), hbm),
        scratch_shapes=[
            pltpu.VMEM((buffers, layers * TURNED, lanes), F32),
            dma((tile_rows,)),
        ],
        compiler_params=pltpu.CompilerParams(vmem_limit_bytes=65000 * 2**10),
        name="fields",
    )(turned, spread, weights, increment)
    return increment, alpha_fields


def solution(mesh):
    in_specs = (
        P(("ens", "gx"), None, None, "gy"),
        P(),
        P(("ens", "gx"), "gy"),
        P(None, ("ens", "gx"), "gy"),
        P(None, ("ens", "gx"), "gy"),
        P(None, ("ens", "gx"), "gy"),
    )
    out_specs = (P(None, ("ens", "gx"), "gy"), P(("ens", "gx"), None, None, "gy"))
    sizes = tuple(mesh.shape[axis] for axis in ("ens", "gx", "gy"))
    return jax.shard_map(
        functools.partial(local, sizes),
        mesh=mesh,
        in_specs=in_specs,
        out_specs=out_specs,
        check_vma=False,
    )
```

```python
import functools
import math

import jax
import jax.numpy as jnp
from jax import lax
from jax.experimental import pallas as pl
from jax.experimental.pallas import tpu as pltpu
from jax.sharding import PartitionSpec as P

GRIDS = 3
SWEEPS = 2
COARSE_SWEEPS = 4
ITERATIONS = 3
SUB = 8
LANES = 128
PAIR = 2
TURNED = 16
ROWS = 4
HALF = SUB // 2
TOGETHER = 8

diffusivity = 16.0
damping = 0.8
MESH = pl.DeviceIdType.MESH
F32 = jnp.float32
BF16 = jnp.bfloat16


def strength_of(level):
    return diffusivity / 4.0**level


def lane_index(width):
    return lax.broadcasted_iota(jnp.int32, (SUB, width), 1)


def low_half(width):
    return lax.broadcasted_iota(jnp.int32, (SUB, width), 0) < HALF


def swapped(values):
    return pltpu.roll(values, HALF, 0)


def pack_rows(rows):
    low = low_half(LANES)
    firsts = [jnp.where(low, a, swapped(b)) for a, b in (rows[:2], rows[2:])]
    seconds = [jnp.where(low, swapped(a), b) for a, b in (rows[:2], rows[2:])]
    return [jnp.concatenate(blocks, axis=0).astype(BF16) for blocks in (firsts, seconds)]


def unpack_rows(firsts, seconds):
    low = low_half(LANES)
    firsts, seconds = firsts.astype(F32), seconds.astype(F32)
    rows = []
    for at in (0, SUB):
        a, c = firsts[at : at + SUB], seconds[at : at + SUB]
        rows += [jnp.where(low, a, swapped(c)), jnp.where(low, swapped(a), c)]
    return rows


def join_halves(ref, rows):
    low = low_half(ref.shape[-1])
    ref[0] = jnp.where(low, 0.0, swapped(ref[rows]))
    ref[rows + 1] = jnp.where(low, swapped(ref[1]), 0.0)


def over_rows(count, body):
    chunk = min(SUB, count)

    @pl.loop(0, count // chunk)
    def _(block):
        body(block * chunk, chunk)


def beside(here, step):
    width = here.shape[-1]
    lane = lane_index(width)
    left = jnp.where(lane < step, 0.0, pltpu.roll(here, step, 1))
    right = jnp.where(lane >= width - step, 0.0, pltpu.roll(here, width - step, 1))
    return left + right


def around(loaded, index, step):
    return loaded[index] + loaded[index + 2] + beside(loaded[index + 1], step)


def relax(load, source, dst, rows, level, scale=None):
    strength = strength_of(level)
    factor = damping / (1.0 + 4.0 * strength)
    keep = 1.0 - damping
    spread_by = factor * strength
    if scale is not None:
        keep, spread_by = keep * scale, spread_by * scale

    def body(start, chunk):
        loaded = load(start, chunk)
        for r in range(chunk):
            dst[start + r + 1] = (
                keep * loaded[r + 1]
                + factor * source[start + r + 1]
                + spread_by * around(loaded, r, 2**level)
            )

    over_rows(rows, body)
    join_halves(dst, rows)


def rows_of(ref):
    return lambda start, chunk: [ref[start + r] for r in range(chunk + 2)]


def prolonged(ref, coarse):
    def load(start, chunk):
        extra = [coarse[start // 2 + r] for r in range(chunk // 2 + 2)]
        return [ref[start + r] + extra[(r + 1) // 2] for r in range(chunk + 2)]

    return load


def restrict_remainder(src, source, dst, rows, level):
    strength = strength_of(level)
    step = 2**level

    def body(start, chunk):
        loaded = rows_of(src)(start, chunk)
        over = [
            source[start + r + 1]
            - (1.0 + 4.0 * strength) * loaded[r + 1]
            + strength * around(loaded, r, step)
            for r in range(chunk)
        ]
        for r in range(0, chunk, 2):
            both = over[r] + over[r + 1]
            width = both.shape[-1]
            even = lax.rem(lane_index(width) // step, 2) == 0
            other = jnp.where(even, pltpu.roll(both, width - step, 1), pltpu.roll(both, step, 1))
            dst[start // 2 + r // 2 + 1] = 0.25 * (both + other)

    over_rows(rows, body)
    join_halves(dst, rows // 2)


def vcycle(levels, level, rows):
    source, first, second = levels[level]
    factor = damping / (1.0 + 4.0 * strength_of(level))
    relax(rows_of(source), source, first, rows, level, factor)
    before = COARSE_SWEEPS - 2 if level == GRIDS - 1 else SWEEPS - 2
    for _ in range(before):
        relax(rows_of(first), source, second, rows, level)
        first, second = second, first
    if level == GRIDS - 1:
        return first
    restrict_remainder(first, source, levels[level + 1][0], rows, level)
    coarse = vcycle(levels, level + 1, rows // 2)
    load = prolonged(first, coarse)
    for _ in range(SWEEPS):
        relax(load, source, second, rows, level)
        first, second = second, first
        load = rows_of(first)
    return first


def kernel(
    sizes,
    groups,
    members_in,
    spread,
    sea,
    innovations_in,
    obs_error_in,
    scale_in,
    increment,
    weights,
    turned,
    staged,
    innovations,
    obs_error,
    scale,
    members,
    native,
    turning,
    gathered,
    s_recv,
    e_recv,
    own_sum,
    residual,
    along,
    image,
    cov_dir,
    cov_res,
    ens_res,
    ens_along,
    f_along,
    f_send,
    f_recv,
    b_send,
    back,
    p_recv,
    state,
    blend,
    *rest,
):
    n_ens, n_gx, n_gy = sizes
    level_refs = rest[: 3 * GRIDS]
    (f_ssem, f_rsem, b_ssem, b_rsem, p_ssem, p_rsem, r_ssem, r_rsem, s_ssem, s_rsem, e_rsem, m_sem, i_sem, t_sem, w_sem) = rest[3 * GRIDS :]
    levels = [level_refs[3 * g : 3 * g + 3] for g in range(GRIDS)]
    n_blocks = n_ens * n_gx
    n_dev = n_blocks * n_gy
    my_ens = lax.axis_index("ens")
    my_gx = lax.axis_index("gx")
    block = my_ens * n_gx + my_gx
    column = lax.axis_index("gy")
    me = block * n_gy + column
    next_group = (me * groups + n_dev - 1) // n_dev
    is_owner = (next_group < groups) & (next_group * n_dev // groups == me)
    my_group = jnp.minimum(next_group, groups - 1)
    layers = spread.shape[0]
    tile_rows = innovations.shape[0]
    count = members.shape[0]
    grid_rows = tile_rows * n_blocks
    half_rows = grid_rows // 2
    half_blocks = n_blocks // 2
    eights = -(-layers // SUB)
    quads = tile_rows // ROWS
    parts = tile_rows // PAIR
    together = math.gcd(count, TOGETHER)

    def row_of(field, row):
        return field[row]

    def device(rank):
        return (rank // (n_gx * n_gy), rank // n_gy % n_gx, rank % n_gy)

    def ens_at(step):
        return lax.rem(my_ens + n_ens - step, n_ens)

    def gx_at(hop):
        return lax.rem(my_gx + hop, n_gx)

    def remote(src, dst, send_sem, recv_sem, target):
        pltpu.make_async_remote_copy(
            src_ref=src,
            dst_ref=dst,
            send_sem=send_sem,
            recv_sem=recv_sem,
            device_id=target,
            device_id_type=MESH,
        ).start()

    def each_other(body):
        def one(blocks_on, columns_on):
            there = lax.rem(block + blocks_on, n_blocks)
            at = lax.rem(column + columns_on, n_gy)
            body((there // n_gx, lax.rem(there, n_gx), at), there * n_gy + at)

        for c in range(1, n_gy):
            one(0, c)

        @pl.loop(1, n_blocks)
        def _(blocks_on):
            for c in range(n_gy):
                one(blocks_on, c)

    def done(ref, sem):
        pltpu.make_async_copy(ref, ref, sem).wait()

    def fetch(k):
        return pltpu.make_async_copy(members_in.at[k], native.at[k], m_sem.at[k])

    fields = [
        pltpu.make_async_copy(given.at[:, r, :], field.at[r], i_sem.at[n, r])
        for n, (given, field) in enumerate(
            ((innovations_in, innovations), (scale_in, scale), (obs_error_in, obs_error))
        )
        for r in range(tile_rows)
    ]
    for copy in fields:
        copy.start()

    @pl.loop(0, count)
    def _(k):
        fetch(k).start()

    barrier = pltpu.get_barrier_semaphore()

    each_other(
        lambda there, rank: pl.semaphore_signal(
            barrier, inc=1, device_id=there, device_id_type=MESH
        )
    )

    def pair_rows(pair):
        return pl.ds(pair * PAIR, PAIR)

    def tile_of(iteration, origin, pair):
        return gathered.at[iteration, origin, pair_rows(pair)]

    def part_of(origin, pair):
        return staged.at[pl.ds(origin * tile_rows + pair * PAIR, PAIR)]

    def forward_x(iteration, step, pair):
        origin = ens_at(step) * n_gx + my_gx
        tile = tile_of(iteration, origin, pair)
        for hop in range(1, n_gx):
            remote(
                tile,
                tile,
                r_ssem,
                r_rsem.at[iteration, origin, pair],
                (my_ens, gx_at(hop), column),
            )

    def receive_and_forward(iteration, step, pair):
        origin = ens_at(step) * n_gx + my_gx
        done(tile_of(iteration, origin, pair), r_rsem.at[iteration, origin, pair])
        forward_x(iteration, step, pair)

    def send_tile(iteration, pair):
        tile = tile_of(iteration, block, pair)
        for step in range(1, n_ens):
            remote(
                tile,
                tile,
                r_ssem,
                r_rsem.at[iteration, block, pair],
                (ens_at(n_ens - step), my_gx, column),
            )
        forward_x(iteration, 0, pair)

    def tiles_sent(sem):
        done(gathered.at[0, pl.ds(0, n_blocks - 1)], sem)

    def pack_source(values):
        for eight in range(eights):
            rows = [value[eight * SUB : (eight + 1) * SUB] for value in values]
            if eight * SUB + SUB > layers:
                tail = jnp.zeros((eight * SUB + SUB - layers, LANES), F32)
                rows = [jnp.concatenate([row, tail], axis=0) for row in rows]
            for quad in range(quads):
                blocks = pack_rows(rows[quad * ROWS : (quad + 1) * ROWS])
                for n, packed in enumerate(blocks):
                    f_send[2 * eight + n, quad] = packed

    def slot(rank):
        return pl.ds(rank * quads, quads)

    def but_own(ref, sem):
        @pl.when(is_owner)
        def _():
            done(ref.at[pl.ds(0, groups - 1)], sem)

        @pl.when(jnp.logical_not(is_owner))
        def _():
            done(ref.at[pl.ds(0, groups)], sem)

    def send_source():
        for group in range(groups):
            rank = group * n_dev // groups

            @pl.when(me != rank)
            def _():
                remote(f_send.at[group], f_recv.at[slot(me)], f_ssem, f_rsem, device(rank))

        @pl.when(is_owner)
        def _():
            for quad in range(quads):
                f_recv[me * quads + quad] = f_send[my_group, quad]

    for copy in fields:
        copy.wait()
    for r in range(tile_rows):
        start = row_of(innovations, r)
        residual[r] = start
        gathered[0, block, r] = (sea[r : r + 1].astype(F32) * start).astype(BF16)
        zero = jnp.zeros_like(start)
        for ref in (along, image, cov_dir, ens_res, ens_along, increment):
            ref[r] = zero
    pack_source([row_of(scale, r) * (sea[r : r + 1].astype(F32) * residual[r]) for r in range(tile_rows)])
    for group in range(groups, 2 * eights):
        back[group] = jnp.zeros(back.shape[1:], BF16)
    blend[...] = jnp.zeros_like(blend)
    blend[1, 0] = jnp.ones((1, LANES), F32)
    state[0] = -jnp.ones((1, LANES), F32)
    state[1] = jnp.zeros((1, LANES), F32)
    state[2] = jnp.ones((1, LANES), F32)

    @pl.when(is_owner)
    def _():
        @pl.loop(0, half_rows)
        def _(row):
            f_along[row] = jnp.zeros(f_along.shape[1:], F32)
            levels[0][0][row + 1] = jnp.zeros(f_along.shape[1:], F32)

    def keep(k):
        return pltpu.make_async_copy(members.at[k], turned.at[k], t_sem.at[k])

    def turn(k):
        fetch(k).wait()

        @pl.loop(0, grid_rows // TURNED)
        def _(chunk):
            rows = pl.ds(pl.multiple_of(chunk * TURNED, TURNED), TURNED)
            turning[...] = native[k, :, rows, :].astype(F32).reshape(layers * TURNED, LANES)
            for r in range(TURNED):
                values = turning[pl.ds(r, layers, stride=TURNED), :]
                members[k, chunk * TURNED + r] = values.astype(BF16)

        keep(k).start()

    @pl.loop(0, count // 2)
    def _(k):
        turn(k)

    pl.semaphore_wait(barrier, n_dev - 1)
    for pair in range(parts):
        send_tile(0, pair)
    send_source()

    @pl.loop(count // 2, count)
    def _(k):
        turn(k)

    def members_from(k, first):
        return [[members[k + n, first + r] for r in range(PAIR)] for n in range(together)]

    def mix(members_at, vector):
        product = [
            values * vector[r] for member in members_at for r, values in enumerate(member)
        ]
        mixed = jnp.dot(
            spread[...], jnp.concatenate(product, axis=1), preferred_element_type=F32
        )
        pieces = [mixed[:, n * LANES : (n + 1) * LANES] for n in range(len(product))]
        return [pieces[n : n + PAIR] for n in range(0, len(pieces), PAIR)]

    def partial_sum(iteration, origin, pair, store):
        vector = [gathered[iteration, origin, pair * PAIR + r] for r in range(PAIR)]
        first = origin * tile_rows + pair * PAIR

        def sum_of(k):
            values = members_from(k, first)
            mixed = mix(values, vector)
            sums = []
            for r in range(PAIR):
                running = values[0][r].astype(F32) * mixed[0][r]
                for n in range(1, together):
                    running = running + values[n][r].astype(F32) * mixed[n][r]
                sums.append(running)
            return sums

        sums = sum_of(0)
        for k in range(together, count, together):
            sums = [a + b for a, b in zip(sums, sum_of(k))]
        store(sums)

    def places(quad, c):
        first = ((quad // quads) * n_gy + c) * quads + lax.rem(quad, quads)
        return first, first + half_blocks * n_gy * quads

    def owner_cycle(iteration):
        done(f_recv.at[pl.ds(0, (n_dev - 1) * quads)], f_rsem)
        source = levels[0][0]
        alpha, ratio = state[0], state[1]

        @pl.loop(0, half_rows // ROWS)
        def _(quad):
            for c in range(n_gy):
                lanes = pl.ds(c * LANES, LANES)
                both = [f_recv[at] for at in places(quad, c)]
                for r, new in enumerate(unpack_rows(*both)):
                    row = quad * ROWS + r
                    more = new + ratio * f_along[row, :, lanes]
                    f_along[row, :, lanes] = more
                    source[row + 1, :, lanes] = source[row + 1, :, lanes] - alpha * more

        join_halves(source, half_rows)
        result = vcycle(levels, 0, half_rows)

        @pl.when(iteration > 0)
        def _():
            cycle_sent()

        @pl.loop(0, half_rows // ROWS)
        def _(quad):
            for c in range(n_gy):
                lanes = pl.ds(c * LANES, LANES)
                rows = [result[quad * ROWS + r + 1, :, lanes] for r in range(ROWS)]
                for at, packed in zip(places(quad, c), pack_rows(rows)):
                    b_send[at] = packed

        each_other(
            lambda there, rank: remote(
                b_send.at[slot(rank)], back.at[my_group], b_ssem, b_rsem, there
            )
        )
        for quad in range(quads):
            back[my_group, quad] = b_send[me * quads + quad]

    def cycle_sent():
        done(b_send.at[pl.ds(0, (n_dev - 1) * quads)], b_ssem)

    def finish(iteration):
        others = p_recv.at[iteration, pl.ds(0, n_dev - 1)]
        done(others, p_rsem.at[iteration])
        done(others, p_ssem)
        sums = jnp.sum(jnp.sum(p_recv[iteration], axis=0), axis=1, keepdims=True)
        norm_next, product = (jnp.broadcast_to(sums[n : n + 1], (1, LANES)) for n in range(2))
        ratio = jnp.where(iteration == 0, 0.0, norm_next / state[2])
        alpha = norm_next / (product - ratio * norm_next / state[0])
        state[0] = alpha
        state[1] = ratio
        state[2] = norm_next
        for n in range(ITERATIONS):
            towards = ratio * blend[2, n] + blend[1, n]
            blend[2, n] = towards
            blend[3, n] = blend[3, n] + alpha * towards
            more = jnp.where(iteration + 1 == n, 1.0, 0.0) + ratio * blend[0, n]
            blend[0, n] = more
            blend[1, n] = blend[1, n] - alpha * more
        for r in range(tile_rows):
            more = image[r] + ratio * along[r]
            along[r] = more
            residual[r] = residual[r] - alpha * more
            cov = cov_res[r] + ratio * cov_dir[r]
            cov_dir[r] = cov
            increment[r] = increment[r] + alpha * cov

    def sum_x(step, pair):
        ens = ens_at(step)
        for hop in range(1, n_gx):
            gx = gx_at(hop)
            arrival = s_recv.at[gx, ens, pair_rows(pair)]
            done(arrival, s_rsem.at[gx, ens, pair])
            for r in range(PAIR):
                row = pair * PAIR + r
                own_sum[ens, row] = own_sum[ens, row] + s_recv[gx, ens, row].astype(F32)

        @pl.when(step > 0)
        def _():
            origin = ens * n_gx + my_gx
            for r in range(PAIR):
                row = pair * PAIR + r
                staged[origin * tile_rows + row] = own_sum[ens, row].astype(BF16)
            remote(
                part_of(origin, pair),
                e_recv.at[my_ens, pair_rows(pair)],
                s_ssem,
                e_rsem.at[my_ens, pair],
                (ens, my_gx, column),
            )

    @pl.loop(0, ITERATIONS)
    def _(iteration):
        @pl.loop(1, n_ens)
        def _(step):
            receive_and_forward(iteration, step, 0)

        @pl.loop(0, parts * n_blocks)
        def _(job):
            @pl.when((job == n_blocks + 0) & (iteration > 0))
            def _():
                finish(iteration - 1)

            @pl.when((job == n_blocks + 0) & is_owner)
            def _():
                owner_cycle(iteration)

            pair = job // n_blocks
            inner = lax.rem(job, n_blocks)
            hop = inner // n_ens
            step = lax.rem(inner, n_ens)
            ens, gx = ens_at(step), gx_at(hop)
            origin = ens * n_gx + gx

            @pl.when((hop == 1) & (step > 0) & (pair < parts - 1))
            def _():
                receive_and_forward(iteration, step, pair + 1)

            @pl.when(hop > 0)
            def _():
                done(tile_of(iteration, origin, pair), r_rsem.at[iteration, origin, pair])

            def store(sums):
                @pl.when(hop == 0)
                def _():
                    for r in range(PAIR):
                        own_sum[ens, pair * PAIR + r] = sums[r]

                @pl.when(hop > 0)
                def _():
                    for r in range(PAIR):
                        staged[origin * tile_rows + pair * PAIR + r] = sums[r].astype(BF16)
                    remote(
                        part_of(origin, pair),
                        s_recv.at[my_gx, ens, pair_rows(pair)],
                        s_ssem,
                        s_rsem.at[my_gx, ens, pair],
                        (my_ens, gx, column),
                    )

            partial_sum(iteration, origin, pair, store)

            @pl.when((hop == n_gx - 1) & (pair > 0))
            def _():
                sum_x(step, pair - 1)

        tiles_sent(r_ssem)
        but_own(f_send, f_ssem)

        @pl.loop(0, n_ens)
        def _(step):
            sum_x(lax.rem(step + 1, n_ens), parts - 1)

        but_own(back, b_rsem)
        alpha, ratio = state[0], state[1]
        own = jnp.zeros((1, LANES), F32)
        cross = jnp.zeros((1, LANES), F32)
        cycled = [[] for _ in range(tile_rows)]
        for quad in range(quads):
            for eight in range(eights):
                rows = unpack_rows(back[2 * eight, quad], back[2 * eight + 1, quad])
                for r, row in enumerate(rows):
                    cycled[quad * ROWS + r].append(row)
        cycled = [jnp.concatenate(blocks, axis=0)[:layers] for blocks in cycled]
        sources = []
        for pair in range(parts):
            for step in range(1, n_ens):
                ens = ens_at(step)
                done(e_recv.at[ens, pair_rows(pair)], e_rsem.at[ens, pair])
            for r in range(PAIR):
                row = pair * PAIR + r
                total = own_sum[my_ens, row]
                for step in range(1, n_ens):
                    total = total + e_recv[ens_at(step), row].astype(F32)
                more = total + ratio * ens_along[row]
                ens_along[row] = more
                ens = ens_res[row] - alpha * more
                ens_res[row] = ens
                cov = sea[row : row + 1].astype(F32) * (ens + row_of(scale, row) * cycled[row])
                cov_res[row] = cov
                now = residual[row]
                img = cov + row_of(obs_error, row) * now
                image[row] = img
                masked = sea[row : row + 1].astype(F32) * img
                sources.append(row_of(scale, row) * masked)
                own = own + jnp.sum(now * now, axis=0, keepdims=True)
                cross = cross + jnp.sum(now * img, axis=0, keepdims=True)

                @pl.when(iteration < ITERATIONS - 1)
                def _():
                    gathered[iteration + 1, block, row] = masked.astype(BF16)

            if pair < parts - 1:

                @pl.when(iteration < ITERATIONS - 1)
                def _():
                    send_tile(iteration + 1, pair)

        pack_source(sources)
        p_recv[iteration, me, 0:1] = own
        p_recv[iteration, me, 1:2] = cross

        @pl.when(iteration < ITERATIONS - 1)
        def _():
            send_source()

        mine = p_recv.at[iteration, me]
        each_other(
            lambda there, rank: remote(mine, mine, p_ssem, p_rsem.at[iteration], there)
        )

        @pl.when(iteration < ITERATIONS - 1)
        def _():
            send_tile(iteration + 1, parts - 1)

        tiles_sent(s_ssem)

    finish(ITERATIONS - 1)

    @pl.when(is_owner)
    def _():
        cycle_sent()

    def give(origin):
        return pltpu.make_async_copy(
            own_sum.at[lax.rem(origin, n_ens)],
            weights.at[pl.ds(origin * tile_rows, tile_rows)],
            w_sem.at[lax.rem(origin, n_ens)],
        )

    @pl.loop(0, n_blocks)
    def _(origin):
        held = lax.rem(origin, n_ens)

        @pl.when(origin >= n_ens)
        def _():
            give(origin - n_ens).wait()

        for r in range(tile_rows):
            own_sum[held, r] = sum(
                blend[3, n] * gathered[n, origin, r].astype(F32) for n in range(ITERATIONS)
            )
        give(origin).start()

    @pl.loop(n_blocks - n_ens, n_blocks)
    def _(origin):
        give(origin).wait()

    @pl.loop(0, count)
    def _(k):
        keep(k).wait()


def fields_kernel(members, spread, weights, increment, alpha_fields, increment_out, turning, sem):
    layers = spread.shape[0]
    rows = members.shape[1]
    copies = [
        pltpu.make_async_copy(increment.at[r], increment_out.at[:, r, :], sem.at[r])
        for r in range(increment.shape[0])
    ]

    @pl.when(pl.program_id(0) == 0)
    def _():
        for copy in copies:
            copy.start()

    buffers = turning.shape[0]
    chunks = rows // (TURNED * buffers)

    @pl.loop(0, members.shape[0] * chunks)
    def _(job):
        m, chunk = job // chunks, lax.rem(job, chunks)
        for n in range(buffers):
            first = pl.multiple_of((chunk * buffers + n) * TURNED, TURNED)
            product = [
                (members[m, first + r].astype(F32) * weights[first + r]).astype(BF16)
                for r in range(TURNED)
            ]
            mixed = jnp.dot(
                spread[...], jnp.concatenate(product, axis=1), preferred_element_type=F32
            )
            for r in range(TURNED):
                turning[n, pl.ds(r, layers, stride=TURNED), :] = mixed[:, r * LANES : (r + 1) * LANES]
            alpha_fields[m, :, pl.ds(first, TURNED), :] = (
                turning[n].reshape(layers, TURNED, LANES).astype(BF16)
            )

    @pl.when(pl.program_id(0) == pl.num_programs(0) - 1)
    def _():
        for copy in copies:
            copy.wait()


def local(sizes, members, spread, sea_mask, innovations, obs_error, static_scale):
    n_ens, n_gx, n_gy = sizes
    n_blocks = n_ens * n_gx
    n_dev = n_blocks * n_gy
    count, layers, rows, lanes = members.shape
    tile_rows = innovations.shape[1]
    parts = tile_rows // PAIR
    half_rows = rows // 2
    groups = -(-layers // HALF)
    eights = -(-layers // SUB)
    quads = tile_rows // ROWS
    width = lanes * n_gy

    tile = (tile_rows, layers, lanes)
    f_tile = pltpu.VMEM(tile, F32)
    packed = (ROWS * HALF, lanes)
    scratch = [pltpu.VMEM((rows, layers, lanes), BF16)] + [f_tile] * 3 + [
        pltpu.VMEM((count, rows, layers, lanes), BF16),
        pltpu.VMEM((count, layers, rows, lanes), BF16),
        pltpu.VMEM((layers * TURNED, lanes), F32),
        pltpu.VMEM((ITERATIONS, n_blocks, *tile), BF16),
        pltpu.VMEM((n_gx, n_ens, *tile), BF16),
        pltpu.VMEM((n_ens, *tile), BF16),
        pltpu.VMEM((n_ens, *tile), F32),
    ]
    scratch += [f_tile] * 7
    scratch += [
        pltpu.VMEM((half_rows, SUB, width), F32),
        pltpu.VMEM((2 * eights, quads, *packed), BF16),
        pltpu.VMEM((n_dev * quads, *packed), BF16),
        pltpu.VMEM((n_dev * quads, *packed), BF16),
        pltpu.VMEM((2 * eights, quads, *packed), BF16),
        pltpu.VMEM((ITERATIONS, n_dev, 2, lanes), F32),
        pltpu.VMEM((3, 1, lanes), F32),
        pltpu.VMEM((4, ITERATIONS, 1, lanes), F32),
    ]
    for level in range(GRIDS):
        scratch += [pltpu.VMEM((half_rows // 2**level + 2, SUB, width), F32)] * 3
    dma = pltpu.SemaphoreType.DMA
    scratch += [
        dma(()),
        dma(()),
        dma(()),
        dma(()),
        dma(()),
        dma((ITERATIONS,)),
        dma(()),
        dma((ITERATIONS, n_blocks, parts)),
        dma(()),
        dma((n_gx, n_ens, parts)),
        dma((n_ens, parts)),
        dma((count,)),
        dma((3, tile_rows)),
        dma((count,)),
        dma((n_ens,)),
    ]
    vmem = pl.BlockSpec(memory_space=pltpu.VMEM)
    hbm = pl.BlockSpec(memory_space=pl.ANY)
    increment, weights, turned = pl.pallas_call(
        functools.partial(kernel, sizes, groups),
        out_shape=(
            jax.ShapeDtypeStruct(tile, F32),
            jax.ShapeDtypeStruct((rows, layers, lanes), F32),
            jax.ShapeDtypeStruct((count, rows, layers, lanes), BF16),
        ),
        in_specs=[hbm, vmem, vmem, hbm, hbm, hbm],
        out_specs=(vmem, hbm, hbm),
        scratch_shapes=scratch,
        compiler_params=pltpu.CompilerParams(
            collective_id=0, has_side_effects=True, vmem_limit_bytes=65000 * 2**10
        ),
        name="window",
    )(members, spread, sea_mask, innovations, obs_error, static_scale)
    buffers = math.gcd(rows // TURNED, 2)
    held = math.gcd(count, 2)

    def whole(shape):
        return pl.BlockSpec(shape, lambda k: (0,) * len(shape))

    alpha_fields, increment = pl.pallas_call(
        fields_kernel,
        grid=(count // held,),
        out_shape=(
            jax.ShapeDtypeStruct((count, layers, rows, lanes), BF16),
            jax.ShapeDtypeStruct((layers, tile_rows, lanes), F32),
        ),
        in_specs=[
            pl.BlockSpec((held, rows, layers, lanes), lambda k: (k, 0, 0, 0)),
            whole((layers, layers)),
            whole((rows, layers, lanes)),
            whole(tile),
        ],
        out_specs=(pl.BlockSpec((held, layers, rows, lanes), lambda k: (k, 0, 0, 0)), hbm),
        scratch_shapes=[
            pltpu.VMEM((buffers, layers * TURNED, lanes), F32),
            dma((tile_rows,)),
        ],
        compiler_params=pltpu.CompilerParams(vmem_limit_bytes=65000 * 2**10),
        name="fields",
    )(turned, spread, weights, increment)
    return increment, alpha_fields


def solution(mesh):
    in_specs = (
        P(("ens", "gx"), None, None, "gy"),
        P(),
        P(("ens", "gx"), "gy"),
        P(None, ("ens", "gx"), "gy"),
        P(None, ("ens", "gx"), "gy"),
        P(None, ("ens", "gx"), "gy"),
    )
    out_specs = (P(None, ("ens", "gx"), "gy"), P(("ens", "gx"), None, None, "gy"))
    sizes = tuple(mesh.shape[axis] for axis in ("ens", "gx", "gy"))
    return jax.shard_map(
        functools.partial(local, sizes),
        mesh=mesh,
        in_specs=in_specs,
        out_specs=out_specs,
        check_vma=False,
    )
```

```python
import functools
import math

import jax
import jax.numpy as jnp
from jax import lax
from jax.experimental import pallas as pl
from jax.experimental.pallas import tpu as pltpu
from jax.sharding import PartitionSpec as P

GRIDS = 3
SWEEPS = 2
COARSE_SWEEPS = 4
ITERATIONS = 3
SUB = 8
LANES = 128
PAIR = 2
TURNED = 16
ROWS = 4
HALF = SUB // 2
TOGETHER = 8

diffusivity = 16.0
damping = 0.8
MESH = pl.DeviceIdType.MESH
F32 = jnp.float32
BF16 = jnp.bfloat16


def strength_of(level):
    return diffusivity / 4.0**level


def lane_index(width):
    return lax.broadcasted_iota(jnp.int32, (SUB, width), 1)


def low_half(width):
    return lax.broadcasted_iota(jnp.int32, (SUB, width), 0) < HALF


def swapped(values):
    return pltpu.roll(values, HALF, 0)


def pack_rows(rows):
    low = low_half(LANES)
    firsts = [jnp.where(low, a, swapped(b)) for a, b in (rows[:2], rows[2:])]
    seconds = [jnp.where(low, swapped(a), b) for a, b in (rows[:2], rows[2:])]
    return [jnp.concatenate(blocks, axis=0).astype(BF16) for blocks in (firsts, seconds)]


def unpack_rows(firsts, seconds):
    low = low_half(LANES)
    firsts, seconds = firsts.astype(F32), seconds.astype(F32)
    rows = []
    for at in (0, SUB):
        a, c = firsts[at : at + SUB], seconds[at : at + SUB]
        rows += [jnp.where(low, a, swapped(c)), jnp.where(low, swapped(a), c)]
    return rows


def join_halves(ref, rows):
    low = low_half(ref.shape[-1])
    ref[0] = jnp.where(low, 0.0, swapped(ref[rows]))
    ref[rows + 1] = jnp.where(low, swapped(ref[1]), 0.0)


def over_rows(count, body):
    chunk = min(2 * SUB, count)

    @pl.loop(0, count // chunk)
    def _(block):
        body(block * chunk, chunk)


def beside(here, step):
    width = here.shape[-1]
    lane = lane_index(width)
    left = jnp.where(lane < step, 0.0, pltpu.roll(here, step, 1))
    right = jnp.where(lane >= width - step, 0.0, pltpu.roll(here, width - step, 1))
    return left + right


def around(loaded, index, step):
    return loaded[index] + loaded[index + 2] + beside(loaded[index + 1], step)


def relax(load, source, dst, rows, level, scale=None):
    strength = strength_of(level)
    factor = damping / (1.0 + 4.0 * strength)
    keep = 1.0 - damping
    spread_by = factor * strength
    if scale is not None:
        keep, spread_by = keep * scale, spread_by * scale

    def body(start, chunk):
        loaded = load(start, chunk)
        for r in range(chunk):
            dst[start + r + 1] = (
                keep * loaded[r + 1]
                + factor * source[start + r + 1]
                + spread_by * around(loaded, r, 2**level)
            )

    over_rows(rows, body)
    join_halves(dst, rows)


def rows_of(ref):
    return lambda start, chunk: [ref[start + r] for r in range(chunk + 2)]


def prolonged(ref, coarse):
    def load(start, chunk):
        extra = [coarse[start // 2 + r] for r in range(chunk // 2 + 2)]
        return [ref[start + r] + extra[(r + 1) // 2] for r in range(chunk + 2)]

    return load


def restrict_remainder(src, source, dst, rows, level):
    strength = strength_of(level)
    step = 2**level

    def body(start, chunk):
        loaded = rows_of(src)(start, chunk)
        over = [
            source[start + r + 1]
            - (1.0 + 4.0 * strength) * loaded[r + 1]
            + strength * around(loaded, r, step)
            for r in range(chunk)
        ]
        for r in range(0, chunk, 2):
            both = over[r] + over[r + 1]
            width = both.shape[-1]
            even = lax.rem(lane_index(width) // step, 2) == 0
            other = jnp.where(even, pltpu.roll(both, width - step, 1), pltpu.roll(both, step, 1))
            dst[start // 2 + r // 2 + 1] = 0.25 * (both + other)

    over_rows(rows, body)
    join_halves(dst, rows // 2)


def vcycle(levels, level, rows):
    source, first, second = levels[level]
    factor = damping / (1.0 + 4.0 * strength_of(level))
    relax(rows_of(source), source, first, rows, level, factor)
    before = COARSE_SWEEPS - 2 if level == GRIDS - 1 else SWEEPS - 2
    for _ in range(before):
        relax(rows_of(first), source, second, rows, level)
        first, second = second, first
    if level == GRIDS - 1:
        return first
    restrict_remainder(first, source, levels[level + 1][0], rows, level)
    coarse = vcycle(levels, level + 1, rows // 2)
    load = prolonged(first, coarse)
    for _ in range(SWEEPS):
        relax(load, source, second, rows, level)
        first, second = second, first
        load = rows_of(first)
    return first


def kernel(
    sizes,
    groups,
    members_in,
    spread,
    sea,
    innovations_in,
    obs_error_in,
    scale_in,
    increment,
    weights,
    turned,
    staged,
    innovations,
    obs_error,
    scale,
    members,
    native,
    turning,
    gathered,
    s_recv,
    e_recv,
    own_sum,
    residual,
    along,
    image,
    cov_dir,
    cov_res,
    ens_res,
    ens_along,
    f_along,
    f_send,
    f_recv,
    b_send,
    back,
    p_recv,
    state,
    blend,
    *rest,
):
    n_ens, n_gx, n_gy = sizes
    level_refs = rest[: 3 * GRIDS]
    (f_ssem, f_rsem, b_ssem, b_rsem, p_ssem, p_rsem, r_ssem, r_rsem, s_ssem, s_rsem, e_rsem, m_sem, i_sem, t_sem, w_sem) = rest[3 * GRIDS :]
    levels = [level_refs[3 * g : 3 * g + 3] for g in range(GRIDS)]
    n_blocks = n_ens * n_gx
    n_dev = n_blocks * n_gy
    my_ens = lax.axis_index("ens")
    my_gx = lax.axis_index("gx")
    block = my_ens * n_gx + my_gx
    column = lax.axis_index("gy")
    me = block * n_gy + column
    next_group = (me * groups + n_dev - 1) // n_dev
    is_owner = (next_group < groups) & (next_group * n_dev // groups == me)
    my_group = jnp.minimum(next_group, groups - 1)
    layers = spread.shape[0]
    tile_rows = innovations.shape[0]
    count = members.shape[0]
    grid_rows = tile_rows * n_blocks
    half_rows = grid_rows // 2
    half_blocks = n_blocks // 2
    eights = -(-layers // SUB)
    quads = tile_rows // ROWS
    parts = tile_rows // PAIR
    together = math.gcd(count, TOGETHER)

    def row_of(field, row):
        return field[row]

    def device(rank):
        return (rank // (n_gx * n_gy), rank // n_gy % n_gx, rank % n_gy)

    def ens_at(step):
        return lax.rem(my_ens + n_ens - step, n_ens)

    def gx_at(hop):
        return lax.rem(my_gx + hop, n_gx)

    def remote(src, dst, send_sem, recv_sem, target):
        pltpu.make_async_remote_copy(
            src_ref=src,
            dst_ref=dst,
            send_sem=send_sem,
            recv_sem=recv_sem,
            device_id=target,
            device_id_type=MESH,
        ).start()

    def each_other(body):
        def one(blocks_on, columns_on):
            there = lax.rem(block + blocks_on, n_blocks)
            at = lax.rem(column + columns_on, n_gy)
            body((there // n_gx, lax.rem(there, n_gx), at), there * n_gy + at)

        for c in range(1, n_gy):
            one(0, c)

        @pl.loop(1, n_blocks)
        def _(blocks_on):
            for c in range(n_gy):
                one(blocks_on, c)

    def done(ref, sem):
        pltpu.make_async_copy(ref, ref, sem).wait()

    def fetch(k):
        return pltpu.make_async_copy(members_in.at[k], native.at[k], m_sem.at[k])

    fields = [
        pltpu.make_async_copy(given.at[:, r, :], field.at[r], i_sem.at[n, r])
        for n, (given, field) in enumerate(
            ((innovations_in, innovations), (scale_in, scale), (obs_error_in, obs_error))
        )
        for r in range(tile_rows)
    ]
    for copy in fields:
        copy.start()

    @pl.loop(0, count)
    def _(k):
        fetch(k).start()

    barrier = pltpu.get_barrier_semaphore()

    each_other(
        lambda there, rank: pl.semaphore_signal(
            barrier, inc=1, device_id=there, device_id_type=MESH
        )
    )

    def pair_rows(pair):
        return pl.ds(pair * PAIR, PAIR)

    def tile_of(iteration, origin, pair):
        return gathered.at[iteration, origin, pair_rows(pair)]

    def part_of(origin, pair):
        return staged.at[pl.ds(origin * tile_rows + pair * PAIR, PAIR)]

    def forward_x(iteration, step, pair):
        origin = ens_at(step) * n_gx + my_gx
        tile = tile_of(iteration, origin, pair)
        for hop in range(1, n_gx):
            remote(
                tile,
                tile,
                r_ssem,
                r_rsem.at[iteration, origin, pair],
                (my_ens, gx_at(hop), column),
            )

    def receive_and_forward(iteration, step, pair):
        origin = ens_at(step) * n_gx + my_gx
        done(tile_of(iteration, origin, pair), r_rsem.at[iteration, origin, pair])
        forward_x(iteration, step, pair)

    def send_tile(iteration, pair):
        tile = tile_of(iteration, block, pair)
        for step in range(1, n_ens):
            remote(
                tile,
                tile,
                r_ssem,
                r_rsem.at[iteration, block, pair],
                (ens_at(n_ens - step), my_gx, column),
            )
        forward_x(iteration, 0, pair)

    def tiles_sent(sem):
        done(gathered.at[0, pl.ds(0, n_blocks - 1)], sem)

    def pack_source(values):
        for eight in range(eights):
            rows = [value[eight * SUB : (eight + 1) * SUB] for value in values]
            if eight * SUB + SUB > layers:
                tail = jnp.zeros((eight * SUB + SUB - layers, LANES), F32)
                rows = [jnp.concatenate([row, tail], axis=0) for row in rows]
            for quad in range(quads):
                blocks = pack_rows(rows[quad * ROWS : (quad + 1) * ROWS])
                for n, packed in enumerate(blocks):
                    f_send[2 * eight + n, quad] = packed

    def slot(rank):
        return pl.ds(rank * quads, quads)

    def but_own(ref, sem):
        @pl.when(is_owner)
        def _():
            done(ref.at[pl.ds(0, groups - 1)], sem)

        @pl.when(jnp.logical_not(is_owner))
        def _():
            done(ref.at[pl.ds(0, groups)], sem)

    def send_source():
        for group in range(groups):
            rank = group * n_dev // groups

            @pl.when(me != rank)
            def _():
                remote(f_send.at[group], f_recv.at[slot(me)], f_ssem, f_rsem, device(rank))

        @pl.when(is_owner)
        def _():
            for quad in range(quads):
                f_recv[me * quads + quad] = f_send[my_group, quad]

    for copy in fields:
        copy.wait()
    for r in range(tile_rows):
        start = row_of(innovations, r)
        residual[r] = start
        gathered[0, block, r] = (sea[r : r + 1].astype(F32) * start).astype(BF16)
        zero = jnp.zeros_like(start)
        for ref in (along, image, cov_dir, ens_res, ens_along, increment):
            ref[r] = zero
    pack_source([row_of(scale, r) * (sea[r : r + 1].astype(F32) * residual[r]) for r in range(tile_rows)])
    for group in range(groups, 2 * eights):
        back[group] = jnp.zeros(back.shape[1:], BF16)
    blend[...] = jnp.zeros_like(blend)
    blend[1, 0] = jnp.ones((1, LANES), F32)
    state[0] = -jnp.ones((1, LANES), F32)
    state[1] = jnp.zeros((1, LANES), F32)
    state[2] = jnp.ones((1, LANES), F32)

    @pl.when(is_owner)
    def _():
        @pl.loop(0, half_rows)
        def _(row):
            f_along[row] = jnp.zeros(f_along.shape[1:], F32)
            levels[0][0][row + 1] = jnp.zeros(f_along.shape[1:], F32)

    def keep(k):
        return pltpu.make_async_copy(members.at[k], turned.at[k], t_sem.at[k])

    def turn(k):
        fetch(k).wait()

        @pl.loop(0, grid_rows // TURNED)
        def _(chunk):
            rows = pl.ds(pl.multiple_of(chunk * TURNED, TURNED), TURNED)
            turning[...] = native[k, :, rows, :].astype(F32).reshape(layers * TURNED, LANES)
            for r in range(TURNED):
                values = turning[pl.ds(r, layers, stride=TURNED), :]
                members[k, chunk * TURNED + r] = values.astype(BF16)

        keep(k).start()

    @pl.loop(0, count // 2)
    def _(k):
        turn(k)

    pl.semaphore_wait(barrier, n_dev - 1)
    for pair in range(parts):
        send_tile(0, pair)
    send_source()

    @pl.loop(count // 2, count)
    def _(k):
        turn(k)

    def members_from(k, first):
        return [[members[k + n, first + r] for r in range(PAIR)] for n in range(together)]

    def mix(members_at, vector):
        product = [
            values * vector[r] for member in members_at for r, values in enumerate(member)
        ]
        mixed = jnp.dot(
            spread[...], jnp.concatenate(product, axis=1), preferred_element_type=F32
        )
        pieces = [mixed[:, n * LANES : (n + 1) * LANES] for n in range(len(product))]
        return [pieces[n : n + PAIR] for n in range(0, len(pieces), PAIR)]

    def partial_sum(iteration, origin, pair, store):
        vector = [gathered[iteration, origin, pair * PAIR + r] for r in range(PAIR)]
        first = origin * tile_rows + pair * PAIR

        def sum_of(k):
            values = members_from(k, first)
            mixed = mix(values, vector)
            sums = []
            for r in range(PAIR):
                running = values[0][r].astype(F32) * mixed[0][r]
                for n in range(1, together):
                    running = running + values[n][r].astype(F32) * mixed[n][r]
                sums.append(running)
            return sums

        sums = sum_of(0)
        for k in range(together, count, together):
            sums = [a + b for a, b in zip(sums, sum_of(k))]
        store(sums)

    def places(quad, c):
        first = ((quad // quads) * n_gy + c) * quads + lax.rem(quad, quads)
        return first, first + half_blocks * n_gy * quads

    def owner_cycle(iteration):
        done(f_recv.at[pl.ds(0, (n_dev - 1) * quads)], f_rsem)
        source = levels[0][0]
        alpha, ratio = state[0], state[1]

        @pl.loop(0, half_rows // ROWS)
        def _(quad):
            for c in range(n_gy):
                lanes = pl.ds(c * LANES, LANES)
                both = [f_recv[at] for at in places(quad, c)]
                for r, new in enumerate(unpack_rows(*both)):
                    row = quad * ROWS + r
                    more = new + ratio * f_along[row, :, lanes]
                    f_along[row, :, lanes] = more
                    source[row + 1, :, lanes] = source[row + 1, :, lanes] - alpha * more

        join_halves(source, half_rows)
        result = vcycle(levels, 0, half_rows)

        @pl.when(iteration > 0)
        def _():
            cycle_sent()

        @pl.loop(0, half_rows // ROWS)
        def _(quad):
            for c in range(n_gy):
                lanes = pl.ds(c * LANES, LANES)
                rows = [result[quad * ROWS + r + 1, :, lanes] for r in range(ROWS)]
                for at, packed in zip(places(quad, c), pack_rows(rows)):
                    b_send[at] = packed

        each_other(
            lambda there, rank: remote(
                b_send.at[slot(rank)], back.at[my_group], b_ssem, b_rsem, there
            )
        )
        for quad in range(quads):
            back[my_group, quad] = b_send[me * quads + quad]

    def cycle_sent():
        done(b_send.at[pl.ds(0, (n_dev - 1) * quads)], b_ssem)

    def finish(iteration):
        others = p_recv.at[iteration, pl.ds(0, n_dev - 1)]
        done(others, p_rsem.at[iteration])
        done(others, p_ssem)
        sums = jnp.sum(jnp.sum(p_recv[iteration], axis=0), axis=1, keepdims=True)
        norm_next, product = (jnp.broadcast_to(sums[n : n + 1], (1, LANES)) for n in range(2))
        ratio = jnp.where(iteration == 0, 0.0, norm_next / state[2])
        alpha = norm_next / (product - ratio * norm_next / state[0])
        state[0] = alpha
        state[1] = ratio
        state[2] = norm_next
        for n in range(ITERATIONS):
            towards = ratio * blend[2, n] + blend[1, n]
            blend[2, n] = towards
            blend[3, n] = blend[3, n] + alpha * towards
            more = jnp.where(iteration + 1 == n, 1.0, 0.0) + ratio * blend[0, n]
            blend[0, n] = more
            blend[1, n] = blend[1, n] - alpha * more
        for r in range(tile_rows):
            more = image[r] + ratio * along[r]
            along[r] = more
            residual[r] = residual[r] - alpha * more
            cov = cov_res[r] + ratio * cov_dir[r]
            cov_dir[r] = cov
            increment[r] = increment[r] + alpha * cov

    def sum_x(step, pair):
        ens = ens_at(step)
        for hop in range(1, n_gx):
            gx = gx_at(hop)
            arrival = s_recv.at[gx, ens, pair_rows(pair)]
            done(arrival, s_rsem.at[gx, ens, pair])
            for r in range(PAIR):
                row = pair * PAIR + r
                own_sum[ens, row] = own_sum[ens, row] + s_recv[gx, ens, row].astype(F32)

        @pl.when(step > 0)
        def _():
            origin = ens * n_gx + my_gx
            for r in range(PAIR):
                row = pair * PAIR + r
                staged[origin * tile_rows + row] = own_sum[ens, row].astype(BF16)
            remote(
                part_of(origin, pair),
                e_recv.at[my_ens, pair_rows(pair)],
                s_ssem,
                e_rsem.at[my_ens, pair],
                (ens, my_gx, column),
            )

    @pl.loop(0, ITERATIONS)
    def _(iteration):
        @pl.loop(1, n_ens)
        def _(step):
            receive_and_forward(iteration, step, 0)

        @pl.loop(0, parts * n_blocks)
        def _(job):
            @pl.when((job == n_blocks + 0) & (iteration > 0))
            def _():
                finish(iteration - 1)

            @pl.when((job == n_blocks + 0) & is_owner)
            def _():
                owner_cycle(iteration)

            pair = job // n_blocks
            inner = lax.rem(job, n_blocks)
            hop = inner // n_ens
            step = lax.rem(inner, n_ens)
            ens, gx = ens_at(step), gx_at(hop)
            origin = ens * n_gx + gx

            @pl.when((hop == 1) & (step > 0) & (pair < parts - 1))
            def _():
                receive_and_forward(iteration, step, pair + 1)

            @pl.when(hop > 0)
            def _():
                done(tile_of(iteration, origin, pair), r_rsem.at[iteration, origin, pair])

            def store(sums):
                @pl.when(hop == 0)
                def _():
                    for r in range(PAIR):
                        own_sum[ens, pair * PAIR + r] = sums[r]

                @pl.when(hop > 0)
                def _():
                    for r in range(PAIR):
                        staged[origin * tile_rows + pair * PAIR + r] = sums[r].astype(BF16)
                    remote(
                        part_of(origin, pair),
                        s_recv.at[my_gx, ens, pair_rows(pair)],
                        s_ssem,
                        s_rsem.at[my_gx, ens, pair],
                        (my_ens, gx, column),
                    )

            partial_sum(iteration, origin, pair, store)

            @pl.when((hop == n_gx - 1) & (pair > 0))
            def _():
                sum_x(step, pair - 1)

        tiles_sent(r_ssem)
        but_own(f_send, f_ssem)

        @pl.loop(0, n_ens)
        def _(step):
            sum_x(lax.rem(step + 1, n_ens), parts - 1)

        but_own(back, b_rsem)
        alpha, ratio = state[0], state[1]
        own = jnp.zeros((1, LANES), F32)
        cross = jnp.zeros((1, LANES), F32)
        cycled = [[] for _ in range(tile_rows)]
        for quad in range(quads):
            for eight in range(eights):
                rows = unpack_rows(back[2 * eight, quad], back[2 * eight + 1, quad])
                for r, row in enumerate(rows):
                    cycled[quad * ROWS + r].append(row)
        cycled = [jnp.concatenate(blocks, axis=0)[:layers] for blocks in cycled]
        sources = []
        for pair in range(parts):
            for step in range(1, n_ens):
                ens = ens_at(step)
                done(e_recv.at[ens, pair_rows(pair)], e_rsem.at[ens, pair])
            for r in range(PAIR):
                row = pair * PAIR + r
                total = own_sum[my_ens, row]
                for step in range(1, n_ens):
                    total = total + e_recv[ens_at(step), row].astype(F32)
                more = total + ratio * ens_along[row]
                ens_along[row] = more
                ens = ens_res[row] - alpha * more
                ens_res[row] = ens
                cov = sea[row : row + 1].astype(F32) * (ens + row_of(scale, row) * cycled[row])
                cov_res[row] = cov
                now = residual[row]
                img = cov + row_of(obs_error, row) * now
                image[row] = img
                masked = sea[row : row + 1].astype(F32) * img
                sources.append(row_of(scale, row) * masked)
                own = own + jnp.sum(now * now, axis=0, keepdims=True)
                cross = cross + jnp.sum(now * img, axis=0, keepdims=True)

                @pl.when(iteration < ITERATIONS - 1)
                def _():
                    gathered[iteration + 1, block, row] = masked.astype(BF16)

            if pair < parts - 1:

                @pl.when(iteration < ITERATIONS - 1)
                def _():
                    send_tile(iteration + 1, pair)

        pack_source(sources)
        p_recv[iteration, me, 0:1] = own
        p_recv[iteration, me, 1:2] = cross

        @pl.when(iteration < ITERATIONS - 1)
        def _():
            send_source()

        mine = p_recv.at[iteration, me]
        each_other(
            lambda there, rank: remote(mine, mine, p_ssem, p_rsem.at[iteration], there)
        )

        @pl.when(iteration < ITERATIONS - 1)
        def _():
            send_tile(iteration + 1, parts - 1)

        tiles_sent(s_ssem)

    finish(ITERATIONS - 1)

    @pl.when(is_owner)
    def _():
        cycle_sent()

    def give(origin):
        return pltpu.make_async_copy(
            own_sum.at[lax.rem(origin, n_ens)],
            weights.at[pl.ds(origin * tile_rows, tile_rows)],
            w_sem.at[lax.rem(origin, n_ens)],
        )

    @pl.loop(0, n_blocks)
    def _(origin):
        held = lax.rem(origin, n_ens)

        @pl.when(origin >= n_ens)
        def _():
            give(origin - n_ens).wait()

        for r in range(tile_rows):
            own_sum[held, r] = sum(
                blend[3, n] * gathered[n, origin, r].astype(F32) for n in range(ITERATIONS)
            )
        give(origin).start()

    @pl.loop(n_blocks - n_ens, n_blocks)
    def _(origin):
        give(origin).wait()

    @pl.loop(0, count)
    def _(k):
        keep(k).wait()


def fields_kernel(members, spread, weights, increment, alpha_fields, increment_out, turning, sem):
    layers = spread.shape[0]
    rows = members.shape[1]
    copies = [
        pltpu.make_async_copy(increment.at[r], increment_out.at[:, r, :], sem.at[r])
        for r in range(increment.shape[0])
    ]

    @pl.when(pl.program_id(0) == 0)
    def _():
        for copy in copies:
            copy.start()

    buffers = turning.shape[0]
    chunks = rows // (TURNED * buffers)

    @pl.loop(0, members.shape[0] * chunks)
    def _(job):
        m, chunk = job // chunks, lax.rem(job, chunks)
        for n in range(buffers):
            first = pl.multiple_of((chunk * buffers + n) * TURNED, TURNED)
            product = [
                (members[m, first + r].astype(F32) * weights[first + r]).astype(BF16)
                for r in range(TURNED)
            ]
            mixed = jnp.dot(
                spread[...], jnp.concatenate(product, axis=1), preferred_element_type=F32
            )
            for r in range(TURNED):
                turning[n, pl.ds(r, layers, stride=TURNED), :] = mixed[:, r * LANES : (r + 1) * LANES]
            alpha_fields[m, :, pl.ds(first, TURNED), :] = (
                turning[n].reshape(layers, TURNED, LANES).astype(BF16)
            )

    @pl.when(pl.program_id(0) == pl.num_programs(0) - 1)
    def _():
        for copy in copies:
            copy.wait()


def local(sizes, members, spread, sea_mask, innovations, obs_error, static_scale):
    n_ens, n_gx, n_gy = sizes
    n_blocks = n_ens * n_gx
    n_dev = n_blocks * n_gy
    count, layers, rows, lanes = members.shape
    tile_rows = innovations.shape[1]
    parts = tile_rows // PAIR
    half_rows = rows // 2
    groups = -(-layers // HALF)
    eights = -(-layers // SUB)
    quads = tile_rows // ROWS
    width = lanes * n_gy

    tile = (tile_rows, layers, lanes)
    f_tile = pltpu.VMEM(tile, F32)
    packed = (ROWS * HALF, lanes)
    scratch = [pltpu.VMEM((rows, layers, lanes), BF16)] + [f_tile] * 3 + [
        pltpu.VMEM((count, rows, layers, lanes), BF16),
        pltpu.VMEM((count, layers, rows, lanes), BF16),
        pltpu.VMEM((layers * TURNED, lanes), F32),
        pltpu.VMEM((ITERATIONS, n_blocks, *tile), BF16),
        pltpu.VMEM((n_gx, n_ens, *tile), BF16),
        pltpu.VMEM((n_ens, *tile), BF16),
        pltpu.VMEM((n_ens, *tile), F32),
    ]
    scratch += [f_tile] * 7
    scratch += [
        pltpu.VMEM((half_rows, SUB, width), F32),
        pltpu.VMEM((2 * eights, quads, *packed), BF16),
        pltpu.VMEM((n_dev * quads, *packed), BF16),
        pltpu.VMEM((n_dev * quads, *packed), BF16),
        pltpu.VMEM((2 * eights, quads, *packed), BF16),
        pltpu.VMEM((ITERATIONS, n_dev, 2, lanes), F32),
        pltpu.VMEM((3, 1, lanes), F32),
        pltpu.VMEM((4, ITERATIONS, 1, lanes), F32),
    ]
    for level in range(GRIDS):
        scratch += [pltpu.VMEM((half_rows // 2**level + 2, SUB, width), F32)] * 3
    dma = pltpu.SemaphoreType.DMA
    scratch += [
        dma(()),
        dma(()),
        dma(()),
        dma(()),
        dma(()),
        dma((ITERATIONS,)),
        dma(()),
        dma((ITERATIONS, n_blocks, parts)),
        dma(()),
        dma((n_gx, n_ens, parts)),
        dma((n_ens, parts)),
        dma((count,)),
        dma((3, tile_rows)),
        dma((count,)),
        dma((n_ens,)),
    ]
    vmem = pl.BlockSpec(memory_space=pltpu.VMEM)
    hbm = pl.BlockSpec(memory_space=pl.ANY)
    increment, weights, turned = pl.pallas_call(
        functools.partial(kernel, sizes, groups),
        out_shape=(
            jax.ShapeDtypeStruct(tile, F32),
            jax.ShapeDtypeStruct((rows, layers, lanes), F32),
            jax.ShapeDtypeStruct((count, rows, layers, lanes), BF16),
        ),
        in_specs=[hbm, vmem, vmem, hbm, hbm, hbm],
        out_specs=(vmem, hbm, hbm),
        scratch_shapes=scratch,
        compiler_params=pltpu.CompilerParams(
            collective_id=0, has_side_effects=True, vmem_limit_bytes=65000 * 2**10
        ),
        name="window",
    )(members, spread, sea_mask, innovations, obs_error, static_scale)
    buffers = math.gcd(rows // TURNED, 2)
    held = math.gcd(count, 2)

    def whole(shape):
        return pl.BlockSpec(shape, lambda k: (0,) * len(shape))

    alpha_fields, increment = pl.pallas_call(
        fields_kernel,
        grid=(count // held,),
        out_shape=(
            jax.ShapeDtypeStruct((count, layers, rows, lanes), BF16),
            jax.ShapeDtypeStruct((layers, tile_rows, lanes), F32),
        ),
        in_specs=[
            pl.BlockSpec((held, rows, layers, lanes), lambda k: (k, 0, 0, 0)),
            whole((layers, layers)),
            whole((rows, layers, lanes)),
            whole(tile),
        ],
        out_specs=(pl.BlockSpec((held, layers, rows, lanes), lambda k: (k, 0, 0, 0)), hbm),
        scratch_shapes=[
            pltpu.VMEM((buffers, layers * TURNED, lanes), F32),
            dma((tile_rows,)),
        ],
        compiler_params=pltpu.CompilerParams(vmem_limit_bytes=65000 * 2**10),
        name="fields",
    )(turned, spread, weights, increment)
    return increment, alpha_fields


def solution(mesh):
    in_specs = (
        P(("ens", "gx"), None, None, "gy"),
        P(),
        P(("ens", "gx"), "gy"),
        P(None, ("ens", "gx"), "gy"),
        P(None, ("ens", "gx"), "gy"),
        P(None, ("ens", "gx"), "gy"),
    )
    out_specs = (P(None, ("ens", "gx"), "gy"), P(("ens", "gx"), None, None, "gy"))
    sizes = tuple(mesh.shape[axis] for axis in ("ens", "gx", "gy"))
    return jax.shard_map(
        functools.partial(local, sizes),
        mesh=mesh,
        in_specs=in_specs,
        out_specs=out_specs,
        check_vma=False,
    )
```
